32 devices in a mesh: replica: 16 (over z, x, core), shard: 2 (over y).
Axes of the slice: x: 2, y: 2, z: 4, core: 2. Of those that a mesh axis runs over, the one named last changes fastest.
Arguments:
- latents: bfloat16 [32, 1024, 1152], P('replica', 'shard'), may hold values from -6 to 6
- conditions: bfloat16 [32, 1152], P('replica'), may hold values from -6 to 6
- cotangent: bfloat16 [32, 1024, 1152], P('replica', 'shard'), may hold values from -6 to 6
- counts: int32 [16], P('replica'), may hold values from 1 to 2, as said below
- w_ada: bfloat16 [1152, 6912], P('shard'), may hold values from -0.1875 to 0.1875
- b_ada: bfloat16 [6912], P('shard'), may hold values from -3 to 3
- w_qkv: bfloat16 [1152, 3456], P('shard'), may hold values from -0.1875 to 0.1875
- b_qv: bfloat16 [2304], P('shard'), may hold values from -3 to 3
- w_proj: bfloat16 [1152, 1152], P('shard'), may hold values from -3.5 to 3.5
- b_proj: bfloat16 [1152], P('shard'), may hold values from -3 to 3
- w_fc1: bfloat16 [1152, 4608], P('shard'), may hold values from -0.1875 to 0.1875
- b_fc1: bfloat16 [4608], P('shard'), may hold values from -3 to 3
- w_fc2: bfloat16 [4608, 1152], P('shard'), may hold values from -0.09375 to 0.09375
- b_fc2: bfloat16 [1152], P('shard'), may hold values from -3 to 3
Outputs:
- output: bfloat16 [32, 1024, 1152], P('replica', 'shard')
- grad_latents: float32 [32, 1024, 1152], P('replica', 'shard')
- grad_conditions: float32 [32, 1152], P('replica')
- grad_w_ada: float32 [1152, 6912], P('shard')
- grad_b_ada: float32 [6912], P('shard')
- grad_w_qkv: float32 [1152, 3456], P('shard')
- grad_b_qv: float32 [2304], P('shard')
- grad_w_proj: float32 [1152, 1152], P('shard')
- grad_b_proj: float32 [1152], P('shard')
- grad_w_fc1: float32 [1152, 4608], P('shard')
- grad_b_fc1: float32 [4608], P('shard')
- grad_w_fc2: float32 [4608, 1152], P('shard')
- grad_b_fc2: float32 [1152], P('shard')
The draws below stay inside these ranges and needn't reach their ends.
Inputs may be any that keep to these rules, and one draw needn't show every extreme that they name: counts[r] live slots on replica r are its slots 0 to counts[r] - 1 of 2; some replica has all 2 live.
All inputs are finite; a program needn't handle non-finite values.
Results may differ from the reference program's by a relative error of at most 0.019.
Values may be sent and summed in bfloat16 or wider, within the bound.
A program may use at most 512 MiB of HBM per device.

```python
import math
import jax
import jax.numpy as jnp
from jax import lax

D = 1152
HEADS = 16
HDIM = 72
FF = 4608
SEQ = 1024
SLOTS = 2
LATENTS = 32
N_REPLICA = 16


def draw_counts(key, part):
    first_key, second_key = jax.random.split(jax.random.fold_in(key, 11))
    drawn = jax.random.randint(first_key, (N_REPLICA,), 1, SLOTS + 1, dtype=jnp.int32)
    position = jax.random.randint(second_key, (), 0, N_REPLICA, dtype=jnp.int32)
    return drawn.at[position].set(SLOTS)


def shard_levels(rng, extent, shards, low, largest):
    def one(dim, blocks):
        steps = jax.random.uniform(jax.random.fold_in(jax.random.fold_in(rng, 6), dim), (blocks,), jnp.float32, low / len(shards), largest / len(shards))
        return jnp.repeat(jnp.exp(steps), extent[dim] // blocks).reshape((-1,) + (1,) * (len(extent) - dim - 1))

    gain = one(*shards[0])
    for cut in shards[1:]:
        gain = gain * one(*cut)
    return gain


def centred(rng, shape, width, bound, pieces=(), held_as=jnp.bfloat16):
    values = width * jax.random.normal(rng, shape, jnp.float32)
    if pieces:
        values = values * shard_levels(rng, shape, pieces, -0.22, 0.18)
    return jnp.clip(values, -bound, bound).astype(held_as)


def setup_inputs(seed: int = 0) -> dict:
    seeds = jax.random.split(jax.random.key(seed), 15)
    return {
        "latents": centred(seeds[0], (LATENTS, SEQ, D), 1.0, 6.0, ((0, 16), (1, 2))),
        "conditions": centred(seeds[1], (LATENTS, D), 1.0, 6.0, ((0, 16),)),
        "cotangent": centred(seeds[2], (LATENTS, SEQ, D), 1.0, 6.0, ((0, 16), (1, 2))),
        "counts": draw_counts(jax.random.fold_in(seeds[14], 71), 0),
        "w_ada": centred(seeds[4], (D, 6 * D), D ** -0.5, 0.1875, ((0, 2),)),
        "b_ada": centred(seeds[5], (6 * D,), 0.5, 3.0, ((0, 2),)),
        "w_qkv": centred(seeds[6], (D, 3 * D), D ** -0.5, 0.1875, ((0, 2),)),
        "b_qv": centred(seeds[7], (2 * D,), 0.5, 3.0, ((0, 2),)),
        "w_proj": centred(seeds[8], (D, D), (max(1, 3 * D // SEQ)) ** -0.5, 3.5, ((0, 2),)),
        "b_proj": centred(seeds[9], (D,), 0.5, 3.0, ((0, 2),)),
        "w_fc1": centred(seeds[10], (D, FF), D ** -0.5, 0.1875, ((0, 2),)),
        "b_fc1": centred(seeds[11], (FF,), 0.5, 3.0, ((0, 2),)),
        "w_fc2": centred(seeds[12], (FF, D), FF ** -0.5, 0.09375, ((0, 2),)),
        "b_fc2": centred(seeds[13], (D,), 0.5, 3.0, ((0, 2),)),
    }


@jax.custom_vjp
def low(v):
    return lax.optimization_barrier(v.astype(jnp.bfloat16)).astype(jnp.float32)

@jax.custom_vjp
def low_back(v):
    return v

def low_keep(v):
    return (low(v), None)

def low_pass(kept, grad):
    return (grad,)

def back_keep(v):
    return (v, None)

def back_low(kept, grad):
    return (low(grad),)
low.defvjp(low_keep, low_pass)
low_back.defvjp(back_keep, back_low)

def matmul_high(left, right):
    return jnp.dot(left, right, precision=lax.Precision.HIGHEST)

def normalize(values):
    centered = values - lax.optimization_barrier(jnp.mean(values, axis=-1, keepdims=True))
    return centered * lax.rsqrt(lax.optimization_barrier(jnp.mean(centered * centered, axis=-1, keepdims=True)) + 1e-06)

def layer_one(params, tokens, condition):
    w_ada, b_ada, w_qkv, b_qv, w_proj, b_proj, w_fc1, b_fc1, w_fc2, b_fc2 = params
    cond_act = low(jax.nn.silu(condition))
    modul = low_back(matmul_high(cond_act[None, :], w_ada)[0] + b_ada)
    shift_a, scale_a, gate_a, shift_m, scale_m, gate_m = jnp.split(modul, 6)
    normed = low(normalize(tokens) * (1.0 + scale_a) + shift_a)
    qkv = matmul_high(normed, w_qkv)
    query = low(low_back(qkv[:, :D] + b_qv[:D]))
    keys = low(low_back(qkv[:, D:2 * D]))
    values = low(low_back(qkv[:, 2 * D:] + b_qv[D:]))
    length = tokens.shape[0]
    query_h = query.reshape(length, HEADS, HDIM)
    keys_h = keys.reshape(length, HEADS, HDIM)
    values_h = values.reshape(length, HEADS, HDIM)
    scores = low_back(jnp.einsum('qhd,khd->hqk', query_h, keys_h, precision=lax.Precision.HIGHEST) * (1.0 / math.sqrt(HDIM)))
    probs = low(jax.nn.softmax(scores, axis=-1))
    attended = jnp.einsum('hqk,khd->qhd', probs, values_h, precision=lax.Precision.HIGHEST).reshape(length, D)
    attended = low(low_back(attended))
    branch_a = low_back(matmul_high(attended, w_proj) + b_proj)
    resid = tokens + gate_a * branch_a
    mixed = low(normalize(resid) * (1.0 + scale_m) + shift_m)
    pre = low_back(matmul_high(mixed, w_fc1) + b_fc1)
    hidden = low(jax.nn.gelu(pre, approximate=True))
    branch_m = low_back(matmul_high(hidden, w_fc2) + b_fc2)
    return resid + gate_m * branch_m

def reference(latents, conditions, cotangent, counts, w_ada, b_ada, w_qkv, b_qv, w_proj, b_proj, w_fc1, b_fc1, w_fc2, b_fc2):
    params = tuple((p.astype(jnp.float32) for p in (w_ada, b_ada, w_qkv, b_qv, w_proj, b_proj, w_fc1, b_fc1, w_fc2, b_fc2)))
    slot_ids = jnp.arange(LATENTS, dtype=jnp.int32)
    live = (slot_ids % SLOTS < counts[slot_ids // SLOTS]).astype(jnp.float32)[:, None, None]
    stepper = jax.checkpoint(layer_one)

    def forward(weights, tokens, conds):

        def turn(carried, item):
            return (carried, stepper(weights, item[0], item[1]))
        _, result = lax.scan(turn, jnp.float32(0.0), (tokens, conds))
        return result
    final, pullback = jax.vjp(forward, params, latents.astype(jnp.float32), conditions.astype(jnp.float32))
    grads, grad_latents, grad_conditions = pullback(cotangent.astype(jnp.float32) * live)
    output = (final * live).astype(jnp.bfloat16)
    return (output, grad_latents, grad_conditions, grads[0], grads[1], grads[2], grads[3], grads[4], grads[5], grads[6], grads[7], grads[8], grads[9])
```

```python
from functools import partial
import math

import jax
import jax.numpy as jnp
from jax import lax
from jax.experimental import pallas as pl
from jax.experimental.pallas import tpu as pltpu
from jax.sharding import PartitionSpec as P

HEADS = 16
HDIM = 72
PADDED = 128
LOG2E = math.log2(math.e)


epsilon = 1e-06


def layer_stats(values):
    centered = values - jnp.mean(values, axis=-1, keepdims=True)
    inverse = lax.rsqrt(jnp.mean(centered * centered, axis=-1, keepdims=True) + epsilon)
    return (centered * inverse, inverse)


def layer_back(normal, inverse, d_normal):
    first_mean = jnp.mean(d_normal, axis=-1, keepdims=True)
    second_mean = jnp.mean(d_normal * normal, axis=-1, keepdims=True)
    return inverse * (d_normal - first_mean - normal * second_mean)


def contract_last(left, right):
    return lax.dot_general(
        left, right, (((1,), (1,)), ((), ())), preferred_element_type=jnp.float32
    )


def forward_product(inputs, whole_pair):
    return (
        jnp.dot(inputs, whole_pair[0], preferred_element_type=jnp.float32),
        whole_pair[1].astype(jnp.float32),
    )


def backward_product(grads, whole_pair):
    return contract_last(grads, whole_pair[0])


def swap_cores(values):
    return lax.ppermute(values, "core", [(0, 1), (1, 0)])


def join_cores(mine, axis):
    theirs = swap_cores(mine)
    first = lax.axis_index("core") == 0
    return jnp.stack(
        [jnp.where(first, mine, theirs), jnp.where(first, theirs, mine)], axis=axis
    )


def gather_rows(weight):
    rows, columns = weight.shape
    cores = lax.axis_size("core")
    part = rows // cores
    mine = lax.dynamic_slice_in_dim(weight, lax.axis_index("core") * part, part, 0)
    pieces = lax.all_gather(mine, "shard", axis=0, tiled=False)
    whole = join_cores(pieces, 1)
    return whole.reshape(rows * lax.axis_size("shard"), columns)


def weight_grad(inputs, grads, after):
    n_shard, n_core = (lax.axis_size("shard"), lax.axis_size("core"))
    terms = lax.dot_general(
        inputs, grads, (((0,), (0,)), ((), ())), preferred_element_type=jnp.float32
    ).astype(jnp.bfloat16)
    rows, columns = terms.shape
    part = rows // (n_shard * n_core)
    terms = terms.reshape(n_shard, n_core, part, columns)
    core = lax.axis_index("core")
    keep = lax.dynamic_index_in_dim(terms, core, 1, keepdims=False)
    send = lax.dynamic_index_in_dim(terms, 1 - core, 1, keepdims=False)
    terms = (keep.astype(jnp.float32) + swap_cores(send).astype(jnp.float32)).astype(jnp.bfloat16)
    terms = lax.psum_scatter(terms, "shard", scatter_dimension=0, tiled=True)
    terms = terms.reshape(part, columns)
    if after is not None:
        terms, _ = lax.optimization_barrier((terms, after))
    total = lax.psum(terms, "chip")
    return total


def finish_grad(total):
    joined = join_cores(total, 0).astype(jnp.float32)
    return joined.reshape(2 * total.shape[0], total.shape[1])


def shards(
    latents,
    conditions,
    cotangent,
    counts,
    w_ada,
    b_ada,
    w_qkv,
    b_qv,
    w_proj,
    b_proj,
    w_fc1,
    b_fc1,
    w_fc2,
    b_fc2,
):
    slots, block, width = latents.shape
    n_rows = slots * block
    scale = 1.0 / math.sqrt(HDIM)
    live = (jnp.arange(slots, dtype=jnp.int32) < counts[0]).astype(jnp.float32)[:, None, None]
    index = lax.axis_index("shard")
    biases = (b_ada, b_qv, b_proj, b_fc1, b_fc2)
    bias_all = lax.all_gather(jnp.concatenate(biases), "shard", axis=0, tiled=False)
    full_bias = []
    start = 0
    for bias in biases:
        size = bias.shape[0]
        full_bias.append(bias_all[:, start : start + size].reshape(-1))
        start += size
    full_qkv = (gather_rows(w_qkv), full_bias[1])
    full_proj = (gather_rows(w_proj), full_bias[2])
    full_fc1 = (gather_rows(w_fc1), full_bias[3])
    full_fc2 = (gather_rows(w_fc2), full_bias[4])
    cond_float = conditions.astype(jnp.float32)
    cond_act = jax.nn.silu(cond_float).astype(jnp.bfloat16)
    ada_rows = w_ada.shape[0]
    ada_length = b_ada.shape[0]
    own_cond = lax.dynamic_slice_in_dim(cond_act, index * ada_rows, ada_rows, 1)
    ada_part = jnp.dot(own_cond, w_ada, preferred_element_type=jnp.float32)
    modul = lax.psum(ada_part, "shard") + full_bias[0].astype(jnp.float32)
    shift_a, scale_a, gate_a, shift_m, scale_m, gate_m = [
        piece[:, None, :] for piece in jnp.split(modul, 6, axis=1)
    ]
    tokens = latents.astype(jnp.float32)
    norm_a, inv_a = layer_stats(tokens)
    normed = (norm_a * (1.0 + scale_a) + shift_a).astype(jnp.bfloat16).reshape(n_rows, width)
    qkv_prod, qv_bias = forward_product(normed, full_qkv)
    query = (
        (qkv_prod[:, :width] + qv_bias[:width])
        .astype(jnp.bfloat16)
        .reshape(slots, block, HEADS, HDIM)
    )
    keys_own = qkv_prod[:, width : 2 * width].astype(jnp.bfloat16).reshape(slots, block, width)
    values_own = (
        (qkv_prod[:, 2 * width :] + qv_bias[width:])
        .astype(jnp.bfloat16)
        .reshape(slots, block, width)
    )
    keys_all, values_all = (
        lax.all_gather(keys_own, "shard", axis=1, tiled=True),
        lax.all_gather(values_own, "shard", axis=1, tiled=True),
    )
    length = keys_all.shape[1]
    keys_h = keys_all.reshape(slots, length, HEADS, HDIM)
    values_h = values_all.reshape(slots, length, HEADS, HDIM)
    scores = (
        jnp.einsum("sqhd,skhd->shqk", query, keys_h, preferred_element_type=jnp.float32) * scale
    )
    top_score = jnp.max(scores, axis=-1, keepdims=True)
    log_total = top_score + jnp.log(jnp.sum(jnp.exp(scores - top_score), axis=-1, keepdims=True))
    probs_low = jnp.exp(scores - log_total).astype(jnp.bfloat16)
    attended = jnp.einsum(
        "shqk,skhd->sqhd", probs_low, values_h, preferred_element_type=jnp.float32
    )
    attended_wide = attended
    attended = attended.astype(jnp.bfloat16).reshape(n_rows, width)
    proj_prod, proj_bias = forward_product(attended, full_proj)
    branch_a = (proj_prod + proj_bias).reshape(slots, block, width)
    resid = tokens + gate_a * branch_a
    norm_m, inv_m = layer_stats(resid)
    mixed = (norm_m * (1.0 + scale_m) + shift_m).astype(jnp.bfloat16).reshape(n_rows, width)
    fc1_prod, fc1_bias = forward_product(mixed, full_fc1)
    activated, gelu_back = jax.vjp(partial(jax.nn.gelu, approximate=True), fc1_prod + fc1_bias)
    hidden = activated.astype(jnp.bfloat16)
    fc2_prod, fc2_bias = forward_product(hidden, full_fc2)
    branch_m = (fc2_prod + fc2_bias).reshape(slots, block, width)
    final = resid + gate_m * branch_m
    output = (final * live).astype(jnp.bfloat16)
    d_out = cotangent.astype(jnp.float32) * live
    d_gate_m = jnp.sum(d_out * branch_m, axis=1)
    d_branch_m = (gate_m * d_out).astype(jnp.bfloat16).reshape(n_rows, width)
    sum_fc2 = weight_grad(hidden, d_branch_m, None)
    bias_fc2 = jnp.sum(d_branch_m, axis=0, dtype=jnp.float32)
    d_hidden = backward_product(d_branch_m, full_fc2)
    d_pre = gelu_back(d_hidden)[0].astype(jnp.bfloat16)
    sum_fc1 = weight_grad(mixed, d_pre, sum_fc2)
    bias_fc1 = jnp.sum(d_pre, axis=0, dtype=jnp.float32)
    d_mixed = backward_product(d_pre, full_fc1).reshape(slots, block, width)
    d_shift_m = jnp.sum(d_mixed, axis=1)
    d_scale_m = jnp.sum(d_mixed * norm_m, axis=1)
    d_resid = d_out + layer_back(norm_m, inv_m, d_mixed * (1.0 + scale_m))
    d_gate_a = jnp.sum(d_resid * branch_a, axis=1)
    d_branch_a = (gate_a * d_resid).astype(jnp.bfloat16).reshape(n_rows, width)
    sum_proj = weight_grad(attended, d_branch_a, sum_fc1)
    bias_proj = jnp.sum(d_branch_a, axis=0, dtype=jnp.float32)
    d_attended = (
        backward_product(d_branch_a, full_proj)
        .astype(jnp.bfloat16)
        .reshape(slots, block, HEADS, HDIM)
    )
    scores = (
        jnp.einsum("sqhd,skhd->shqk", query, keys_h, preferred_element_type=jnp.float32) * scale
    )
    probs = jnp.exp(scores - log_total)
    d_probs = jnp.einsum(
        "sqhd,skhd->shqk", d_attended, values_h, preferred_element_type=jnp.float32
    )
    inner = jnp.sum(d_attended.astype(jnp.float32) * attended_wide, axis=-1)
    inner = jnp.swapaxes(inner, 1, 2)[..., None]
    d_scores = (probs * (d_probs - inner)).astype(jnp.bfloat16)
    d_query = (
        (
            jnp.einsum("shqk,skhd->sqhd", d_scores, keys_h, preferred_element_type=jnp.float32)
            * scale
        )
        .astype(jnp.bfloat16)
        .reshape(n_rows, width)
    )
    key_terms = (
        jnp.einsum("shqk,sqhd->skhd", d_scores, query, preferred_element_type=jnp.float32).reshape(
            slots, length, width
        )
        * scale
    )
    value_terms = jnp.einsum(
        "shqk,sqhd->skhd",
        probs.astype(jnp.bfloat16),
        d_attended,
        preferred_element_type=jnp.float32,
    ).reshape(slots, length, width)
    d_keys, d_values = (
        lax.psum_scatter(
            key_terms.astype(jnp.bfloat16), "shard", scatter_dimension=1, tiled=True
        ).astype(jnp.float32),
        lax.psum_scatter(
            value_terms.astype(jnp.bfloat16), "shard", scatter_dimension=1, tiled=True
        ).astype(jnp.float32),
    )
    d_keys = d_keys.astype(jnp.bfloat16).reshape(n_rows, width)
    d_values = d_values.astype(jnp.bfloat16).reshape(n_rows, width)
    d_qkv = jnp.concatenate([d_query, d_keys, d_values], axis=1)
    qv_terms = jnp.concatenate(
        [jnp.sum(d_query, axis=0, dtype=jnp.float32), jnp.sum(d_values, axis=0, dtype=jnp.float32)]
    )
    sum_qkv = weight_grad(normed, d_qkv, sum_proj)
    d_normed = backward_product(d_qkv, full_qkv).reshape(slots, block, width)
    d_shift_a = jnp.sum(d_normed, axis=1)
    d_scale_a = jnp.sum(d_normed * norm_a, axis=1)
    grad_latents = d_resid + layer_back(norm_a, inv_a, d_normed * (1.0 + scale_a))
    d_modul_part = jnp.concatenate(
        [d_shift_a, d_scale_a, d_gate_a, d_shift_m, d_scale_m, d_gate_m], axis=1
    )
    d_modul = lax.psum(d_modul_part, "shard").astype(jnp.bfloat16)
    cond_all = lax.all_gather(own_cond, ("chip", "core"), axis=0, tiled=True)
    d_modul_all = lax.all_gather(d_modul, ("chip", "core"), axis=0, tiled=True)
    grad_w_ada = lax.dot_general(
        cond_all, d_modul_all, (((0,), (0,)), ((), ())), preferred_element_type=jnp.float32
    )
    grad_b_ada = lax.dynamic_slice_in_dim(
        jnp.sum(d_modul_all, axis=0, dtype=jnp.float32), index * ada_length, ada_length, 0
    )
    d_cond_act = lax.all_gather(contract_last(d_modul, w_ada), "shard", axis=1, tiled=True)
    _, silu_back = jax.vjp(jax.nn.silu, cond_float)
    grad_conditions = silu_back(d_cond_act)[0]
    bias_terms = lax.psum(
        jnp.concatenate([qv_terms, bias_proj, bias_fc1, bias_fc2]), ("chip", "core", "shard")
    )
    bias_grads = []
    start = 0
    for bias in biases[1:]:
        size = bias.shape[0]
        bias_grads.append(
            lax.dynamic_slice_in_dim(bias_terms, start + index * size, size, 0)
        )
        start += size * lax.axis_size("shard")
    return (
        output,
        grad_latents,
        grad_conditions,
        grad_w_ada,
        grad_b_ada,
        finish_grad(sum_qkv),
        bias_grads[0],
        finish_grad(sum_proj),
        bias_grads[1],
        finish_grad(sum_fc1),
        bias_grads[2],
        finish_grad(sum_fc2),
        bias_grads[3],
    )


def contract_first(a,b): return lax.dot_general(a,b,(((0,),(0,)),((),())),preferred_element_type=jnp.float32)

def split_heads(src, dst, first=0):
    rows = src.shape[0]
    for h in range(dst.shape[0]):
        piece = src[:, first + h*HDIM: first + (h+1)*HDIM]
        dst[h] = jnp.concatenate([piece, jnp.zeros((rows, PADDED-HDIM), piece.dtype)], axis=1)

def merge_heads(src, dst):
    for h in range(src.shape[0]):
        dst[:, h*HDIM: (h+1)*HDIM] = src[h][:, :HDIM].astype(dst.dtype)

def attend_kernel(block, q_ref, k_ref, v_ref, o_ref, lse_ref, qh, kh, vh, oh):
    n = q_ref.shape[0]
    scale = LOG2E/math.sqrt(HDIM)
    split_heads(q_ref, qh); split_heads(k_ref, kh); split_heads(v_ref, vh)
    @pl.loop(0, HEADS)
    def _(h):
        k = kh[h]; v = vh[h]
        for b in range(n//block):
            rows = pl.ds(b*block, block)
            s = contract_last(k, qh[h, rows, :])
            top = jnp.max(s, axis=0, keepdims=True)
            p = jnp.exp2((s - top)*scale)
            total = jnp.sum(p, axis=0, keepdims=True)
            lse_ref[h, :, rows] = top*scale + jnp.log2(total)
            o = contract_first(p.astype(jnp.bfloat16), v)
            inv = (1.0/total)
            oh[h, rows, :] = (o * jnp.transpose(inv)).astype(oh.dtype)
    merge_heads(oh, o_ref)

def attend(q,k,v,block=256):
    n,w=q.shape
    return pl.pallas_call(lambda *r: attend_kernel(block,*r),
        out_shape=(jax.ShapeDtypeStruct((n,w),jnp.bfloat16), jax.ShapeDtypeStruct((HEADS,1,n),jnp.float32)),
        in_specs=[pl.BlockSpec(memory_space=pltpu.VMEM)]*3,
        out_specs=(pl.BlockSpec(memory_space=pltpu.VMEM),)*2,
        scratch_shapes=[pltpu.VMEM((HEADS,n,PADDED),jnp.bfloat16)]*4,
        compiler_params=pltpu.CompilerParams(vmem_limit_bytes=56*2**20),
        cost_estimate=pl.CostEstimate(flops=4*n*n*w,bytes_accessed=8*n*w,transcendentals=HEADS*n*n),
    )(q,k,v)

def attend_back_kernel(half, block, q_ref, k_ref, v_ref, a_ref, d_ref, lse_ref, dq_ref, dk_ref, dv_ref, qh, kh, vh, dh, delta, dqh, dkh, dvh):
    n = q_ref.shape[0]
    scale = LOG2E/math.sqrt(HDIM)
    heads = HEADS // 2
    first = half * heads * HDIM
    split_heads(q_ref, qh, first); split_heads(k_ref, kh, first); split_heads(v_ref, vh, first); split_heads(d_ref, dh, first)
    ones = jnp.ones((8, HDIM), jnp.float32)
    for h in range(heads):
        cols = slice(first + h*HDIM, first + (h+1)*HDIM)
        prod = a_ref[:, cols].astype(jnp.float32)*d_ref[:, cols].astype(jnp.float32)
        delta[h] = lax.dot_general(ones, prod, (((1,),(1,)),((),())), preferred_element_type=jnp.float32, precision=lax.Precision.HIGHEST)
    @pl.loop(0, heads)
    def _(h):
        q = qh[h]; d = dh[h]; lse = lse_ref[half * heads + h]; dl = delta[h, 0:1, :]
        dq = None
        for b in range(n//block):
            rows = pl.ds(b*block, block)
            k = kh[h, rows, :]
            s = contract_last(k, q)
            p = jnp.exp2(s*scale - lse)
            dp = contract_last(vh[h, rows, :], d)
            ds = (p*(dp - dl)).astype(jnp.bfloat16)
            dvh[h, rows, :] = jnp.dot(p.astype(jnp.bfloat16), d, preferred_element_type=jnp.float32).astype(jnp.bfloat16)
            dkh[h, rows, :] = (jnp.dot(ds, q, preferred_element_type=jnp.float32)*(1/math.sqrt(HDIM))).astype(jnp.bfloat16)
            t = contract_first(ds, k)
            dq = t if dq is None else dq + t
        dqh[h] = (dq*(1/math.sqrt(HDIM))).astype(jnp.bfloat16)
    merge_heads(dqh, dq_ref); merge_heads(dkh, dk_ref); merge_heads(dvh, dv_ref)

def attend_back(q,k,v,a,d,lse,half,block=512):
    n,w=q.shape
    heads = HEADS // 2
    o=jax.ShapeDtypeStruct((n,w//2),jnp.bfloat16)
    return pl.pallas_call(lambda *r: attend_back_kernel(half,block,*r),
        out_shape=(o,o,o),
        in_specs=[pl.BlockSpec(memory_space=pltpu.VMEM)]*6,
        out_specs=(pl.BlockSpec(memory_space=pltpu.VMEM),)*3,
        scratch_shapes=[pltpu.VMEM((heads,n,PADDED),jnp.bfloat16)]*4+[pltpu.VMEM((heads,8,n),jnp.float32)]+[pltpu.VMEM((heads,n,PADDED),jnp.bfloat16)]*3,
        compiler_params=pltpu.CompilerParams(vmem_limit_bytes=60*2**20),
        cost_estimate=pl.CostEstimate(flops=5*n*n*w,bytes_accessed=13*n*w,transcendentals=heads*n*n),
    )(q,k,v,a,d,lse)


def swap_on(values, axis):
    return lax.ppermute(values, axis, [(0, 1), (1, 0)])


def in_order(mine, theirs, axis_name, axis=0):
    first = lax.axis_index(axis_name) == 0
    return jnp.stack(
        [jnp.where(first, mine, theirs), jnp.where(first, theirs, mine)], axis=axis
    )


def pick(values, index, axis):
    return lax.dynamic_index_in_dim(values, index, axis, keepdims=False)


def after(value, *earlier):
    return lax.optimization_barrier((value,) + earlier)[0]


def fetch_start(weight, *earlier):
    part = weight.shape[0] // 4
    x, c = lax.axis_index("x"), lax.axis_index("core")
    mine = lax.dynamic_slice_in_dim(weight, (x * 2 + c) * part, part, 0)
    return swap_on(after(mine, *earlier) if earlier else mine, "shard")


def fetch_rest(mine):
    beside = swap_on(mine, "x")
    return (mine, beside, swap_on(mine, "core"), swap_on(beside, "core"))


def whole_weight(weight, pieces):
    rows, columns = weight.shape
    part = rows // 4
    s, x, c = lax.axis_index("shard"), lax.axis_index("x"), lax.axis_index("core")
    whole = jnp.concatenate([weight, weight], axis=0)
    base = (1 - s) * rows
    spots = ((x, c), (1 - x, c), (x, 1 - c), (1 - x, 1 - c))
    for piece, (px, pc) in zip(pieces, spots):
        whole = lax.dynamic_update_slice_in_dim(
            whole, piece[:, :columns], base + (px * 2 + pc) * part, 0
        )
    return whole


def add_low(*terms):
    total = terms[0].astype(jnp.float32)
    for term in terms[1:]:
        total = total + term.astype(jnp.float32)
    return total.astype(jnp.bfloat16)


def keep_and_send(values, axis_name, axis):
    index = lax.axis_index(axis_name)
    return add_low(
        pick(values, index, axis), swap_on(pick(values, 1 - index, axis), axis_name)
    )


def z_levels():
    return lax.axis_size("z").bit_length() - 1


def z_bit(level):
    return (lax.axis_index("z") >> level) & 1


def swap_z(values, level):
    size = lax.axis_size("z")
    return lax.ppermute(values, "z", [(i, i ^ (1 << level)) for i in range(size)])


def z_order(values, level):
    theirs = swap_z(values, level)
    low = z_bit(level) == 0
    return jnp.stack([jnp.where(low, values, theirs), jnp.where(low, theirs, values)])


def weight_terms(inputs, grads):
    terms = lax.dot_general(
        inputs, grads, (((0,), (0,)), ((), ())), preferred_element_type=jnp.float32
    ).astype(jnp.bfloat16)
    rows, columns = terms.shape
    return terms.reshape(2, 2, 2, rows // 8, columns)


def over_core(terms):
    return keep_and_send(terms, "core", 1)


def over_shard(terms):
    return keep_and_send(terms, "shard", 0)


def over_x(terms):
    return keep_and_send(terms, "x", 0)


def over_z(terms):
    for level in range(z_levels()):
        rows, columns = terms.shape
        terms = terms.reshape(2, rows // 2, columns)
        bit = z_bit(level)
        terms = add_low(pick(terms, bit, 0), swap_z(pick(terms, 1 - bit, 0), level))
    return terms


def spread_z(piece):
    for level in reversed(range(z_levels())):
        theirs = swap_z(piece, level)
        low = z_bit(level) == 0
        piece = jnp.concatenate(
            [jnp.where(low, piece, theirs), jnp.where(low, theirs, piece)], axis=0
        )
    return piece


def spread(piece):
    pair = in_order(piece, swap_on(piece, "x"), "x")
    whole = in_order(pair, swap_on(pair, "core"), "core")
    return whole.astype(jnp.float32).reshape(4 * piece.shape[0], piece.shape[1])


def pair_shards(
    latents,
    conditions,
    cotangent,
    counts,
    w_ada,
    b_ada,
    w_qkv,
    b_qv,
    w_proj,
    b_proj,
    w_fc1,
    b_fc1,
    w_fc2,
    b_fc2,
):
    slots, block, width = latents.shape
    n_rows = slots * block
    s = lax.axis_index("shard")
    live = (s < counts[0]).astype(jnp.float32)

    qkv_mine = fetch_start(w_qkv)
    biases = (b_ada, b_qv, b_proj, b_fc1, b_fc2)
    packed = jnp.concatenate(biases)
    bias_all = in_order(packed, swap_on(packed, "shard"), "shard")
    full_bias = []
    start = 0
    for bias in biases:
        size = bias.shape[0]
        full_bias.append(bias_all[:, start : start + size].reshape(-1).astype(jnp.float32))
        start += size
    ada_bias, qv_bias, proj_bias, fc1_bias, fc2_bias = full_bias
    cond_float = conditions.astype(jnp.float32)
    cond_act = jax.nn.silu(cond_float).astype(jnp.bfloat16)
    ada_rows = w_ada.shape[0]
    own_cond = lax.dynamic_slice_in_dim(cond_act, s * ada_rows, ada_rows, 1)
    ada_part = jnp.dot(own_cond, w_ada, preferred_element_type=jnp.float32)
    modul = pick(ada_part, s, 0) + swap_on(pick(ada_part, 1 - s, 0), "shard") + ada_bias
    shift_a, scale_a, gate_a, shift_m, scale_m, gate_m = [
        piece[None, :] for piece in jnp.split(modul, 6)
    ]
    own_tokens = pick(latents, s, 0)
    far_tokens = swap_on(after(pick(latents, 1 - s, 0), qkv_mine), "shard")
    qkv_pieces = fetch_rest(qkv_mine)
    fc1_mine = fetch_start(jnp.concatenate([w_fc1, w_proj], axis=1), far_tokens)
    fc1_pieces = fetch_rest(fc1_mine)
    fc2_mine = fetch_start(w_fc2, fc1_mine)
    fc2_pieces = fetch_rest(fc2_mine)
    far_cotangent = swap_on(after(pick(cotangent, 1 - s, 0), fc2_mine), "shard")
    cotangents = jnp.concatenate([pick(cotangent, s, 0), far_cotangent], axis=0)

    full_qkv = whole_weight(w_qkv, qkv_pieces)
    tokens = jnp.concatenate([own_tokens, far_tokens], axis=0).astype(jnp.float32)
    norm_a, inv_a = layer_stats(tokens)
    normed = (norm_a * (1.0 + scale_a) + shift_a).astype(jnp.bfloat16)
    qkv_prod = jnp.dot(normed, full_qkv, preferred_element_type=jnp.float32)
    query = (qkv_prod[:, :width] + qv_bias[:width]).astype(jnp.bfloat16)
    keys = qkv_prod[:, width : 2 * width].astype(jnp.bfloat16)
    values = (qkv_prod[:, 2 * width :] + qv_bias[width:]).astype(jnp.bfloat16)
    query, keys, values, fc1_mine = lax.optimization_barrier((query, keys, values, fc1_mine))
    attended, log_total = attend(query, keys, values, 512)
    full_proj = whole_weight(w_proj, [p[:, w_fc1.shape[1]:] for p in fc1_pieces])
    full_fc1 = whole_weight(w_fc1, fc1_pieces)
    branch_a = jnp.dot(attended, full_proj, preferred_element_type=jnp.float32) + proj_bias
    resid = tokens + gate_a * branch_a
    norm_m, inv_m = layer_stats(resid)
    mixed = (norm_m * (1.0 + scale_m) + shift_m).astype(jnp.bfloat16)
    pre = jnp.dot(mixed, full_fc1, preferred_element_type=jnp.float32) + fc1_bias
    activated, gelu_back = jax.vjp(partial(jax.nn.gelu, approximate=True), pre)
    hidden = activated.astype(jnp.bfloat16)
    full_fc2 = whole_weight(w_fc2, fc2_pieces)
    branch_m = jnp.dot(hidden, full_fc2, preferred_element_type=jnp.float32) + fc2_bias
    out = ((resid + gate_m * branch_m) * live).astype(jnp.bfloat16)
    out_other = swap_on(out[block:], "shard")
    output = in_order(out[:block], out_other, "shard")

    d_out = cotangents.astype(jnp.float32) * live
    d_gate_m = jnp.sum(d_out * branch_m, axis=0)
    d_branch_m = (gate_m * d_out).astype(jnp.bfloat16)
    sum_fc2 = weight_terms(hidden, d_branch_m)
    bias_fc2 = jnp.sum(d_branch_m, axis=0, dtype=jnp.float32)
    d_branch_m = after(d_branch_m, sum_fc2)
    d_pre = gelu_back(contract_last(d_branch_m, full_fc2))[0].astype(jnp.bfloat16)
    sum_fc2 = over_core(sum_fc2)
    d_pre, sum_fc2 = lax.optimization_barrier((d_pre, sum_fc2))
    sum_fc1 = weight_terms(mixed, d_pre)
    bias_fc1 = jnp.sum(d_pre, axis=0, dtype=jnp.float32)
    d_pre, sum_fc1 = lax.optimization_barrier((d_pre, sum_fc1))
    d_mixed = contract_last(d_pre, full_fc1)
    d_shift_m = jnp.sum(d_mixed, axis=0)
    d_scale_m = jnp.sum(d_mixed * norm_m, axis=0)
    d_resid = d_out + layer_back(norm_m, inv_m, d_mixed * (1.0 + scale_m))
    d_gate_a = jnp.sum(d_resid * branch_a, axis=0)
    d_branch_a = (gate_a * d_resid).astype(jnp.bfloat16)
    sum_fc1 = over_core(sum_fc1)
    sum_proj = weight_terms(attended, d_branch_a)
    bias_proj = jnp.sum(d_branch_a, axis=0, dtype=jnp.float32)
    d_attended = contract_last(d_branch_a, full_proj).astype(jnp.bfloat16)
    sum_proj = over_core(sum_proj)
    sum_fc2 = over_shard(sum_fc2)
    sum_fc1 = jnp.concatenate([sum_fc1, sum_proj], axis=-1)
    d_attended, sum_fc2, sum_fc1 = lax.optimization_barrier((d_attended, sum_fc2, sum_fc1))
    first = attend_back(query, keys, values, attended, d_attended, log_total, 0)
    sum_fc2 = over_x(sum_fc2)
    d_attended, sum_fc2, first = lax.optimization_barrier((d_attended, sum_fc2, first))
    sum_qkv = [weight_terms(normed, jnp.concatenate(first, axis=1))]
    d_attended, sum_qkv[0] = lax.optimization_barrier((d_attended, sum_qkv[0]))
    second = attend_back(query, keys, values, attended, d_attended, log_total, 1)
    sum_qkv[0] = over_core(sum_qkv[0])
    sum_fc2 = over_z(sum_fc2)
    sum_fc1 = over_shard(sum_fc1)
    second, sum_qkv[0], sum_fc2, sum_fc1 = lax.optimization_barrier(
        (second, sum_qkv[0], sum_fc2, sum_fc1)
    )
    sum_qkv.append(weight_terms(normed, jnp.concatenate(second, axis=1)))
    d_query, d_keys, d_values = [
        jnp.concatenate(halves, axis=1) for halves in zip(first, second)
    ]
    d_qkv = jnp.concatenate([d_query, d_keys, d_values], axis=1)
    bias_qv = jnp.concatenate(
        [jnp.sum(d_query, axis=0, dtype=jnp.float32), jnp.sum(d_values, axis=0, dtype=jnp.float32)]
    )
    d_qkv, sum_qkv[1] = lax.optimization_barrier((d_qkv, sum_qkv[1]))
    d_normed = contract_last(d_qkv, full_qkv)
    d_shift_a = jnp.sum(d_normed, axis=0)
    d_scale_a = jnp.sum(d_normed * norm_a, axis=0)
    grad_tokens = d_resid + layer_back(norm_a, inv_a, d_normed * (1.0 + scale_a))
    sum_qkv[1] = over_core(sum_qkv[1])
    sum_qkv[0] = over_shard(sum_qkv[0])
    sum_fc1 = over_x(sum_fc1)
    grad_fc2 = spread(spread_z(sum_fc2))
    sum_qkv = jnp.concatenate([over_x(sum_qkv[0]), over_x(over_shard(sum_qkv[1]))], axis=-1)
    grad_qkv = spread(spread_z(over_z(sum_qkv)))
    grad_qkv = jnp.concatenate(
        [
            grad_qkv[:, half * 3 * width // 2 + t * width // 2 :][:, : width // 2]
            for t in range(3)
            for half in range(2)
        ],
        axis=1,
    )
    grad_fc1 = spread(spread_z(over_z(sum_fc1)))
    grad_fc1, grad_proj = grad_fc1[:, : w_fc1.shape[1]], grad_fc1[:, w_fc1.shape[1] :]
    grad_other = swap_on(grad_tokens[block:].astype(jnp.bfloat16), "shard").astype(jnp.float32)
    grad_latents = in_order(grad_tokens[:block], grad_other, "shard")

    d_modul = jnp.concatenate(
        [d_shift_a, d_scale_a, d_gate_a, d_shift_m, d_scale_m, d_gate_m]
    ).astype(jnp.bfloat16)
    row = jnp.concatenate([d_modul, pick(cond_act, s, 0)])
    terms = [t.reshape(2, -1) for t in (bias_qv, bias_proj, bias_fc1, bias_fc2)]
    terms = jnp.concatenate(terms, axis=1)
    sent = jnp.concatenate([row, pick(terms, 1 - s, 0).astype(jnp.bfloat16)])
    came = swap_on(sent, "shard")
    length = row.shape[0]
    table = in_order(row, came[:length], "shard")
    d_modul_pair = table[:, : d_modul.shape[0]]
    total = pick(terms, s, 0) + came[length:].astype(jnp.float32)
    for swap in [
        lambda v: in_order(v, swap_on(v, "core"), "core"),
        lambda v: in_order(v, swap_on(v, "x"), "x"),
    ] + [
        lambda v, level=level: z_order(v, level) for level in range(z_levels())
    ]:
        both = swap(jnp.concatenate([table.reshape(-1), total.astype(jnp.bfloat16)]))
        table = both[:, : table.size].reshape(-1, length)
        total = jnp.sum(both[:, table.size // 2 :].astype(jnp.float32), axis=0)
    d_modul_all, cond_all = table[:, : d_modul.shape[0]], table[:, d_modul.shape[0] :]
    cond_all = lax.dynamic_slice_in_dim(cond_all, s * ada_rows, ada_rows, 1)
    grad_w_ada = lax.dot_general(
        cond_all, d_modul_all, (((0,), (0,)), ((), ())), preferred_element_type=jnp.float32
    )
    ada_length = b_ada.shape[0]
    grad_b_ada = lax.dynamic_slice_in_dim(
        jnp.sum(d_modul_all, axis=0, dtype=jnp.float32), s * ada_length, ada_length, 0
    )
    d_cond = contract_last(d_modul_pair, w_ada)
    d_cond = in_order(d_cond, swap_on(d_cond, "shard"), "shard")
    d_cond_act = jnp.moveaxis(d_cond, 0, 1).reshape(slots, width)
    _, silu_back = jax.vjp(jax.nn.silu, cond_float)
    grad_conditions = silu_back(d_cond_act)[0]
    bias_grads = []
    start = 0
    for bias in biases[1:]:
        size = bias.shape[0]
        bias_grads.append(total[start : start + size])
        start += size
    return (
        output,
        grad_latents,
        grad_conditions,
        grad_w_ada,
        grad_b_ada,
        grad_qkv,
        bias_grads[0],
        grad_proj,
        bias_grads[1],
        grad_fc1,
        bias_grads[2],
        grad_fc2,
        bias_grads[3],
    )


def solution(mesh):
    n_z = mesh.shape["replica"] // 4
    if mesh.shape["shard"] == 2 and n_z & (n_z - 1) == 0 and mesh.shape["replica"] % 4 == 0:
        return pair_solution(mesh)
    return wide_solution(mesh)


def pair_solution(mesh):
    names = mesh.axis_names
    n_replica, n_shard = (mesh.shape["replica"], mesh.shape["shard"])
    devices = mesh.devices.transpose(names.index("replica"), names.index("shard"))
    fine = jax.sharding.Mesh(
        devices.reshape(n_replica // 4, 2, 2, n_shard), ("z", "x", "core", "shard")
    )
    return mapped(pair_shards, fine, ("z", "x", "core"))


def wide_solution(mesh):
    names = mesh.axis_names
    n_replica, n_shard = (mesh.shape["replica"], mesh.shape["shard"])
    devices = mesh.devices.transpose(names.index("replica"), names.index("shard"))
    fine = jax.sharding.Mesh(
        devices.reshape(n_replica // 2, 2, n_shard), ("chip", "core", "shard")
    )
    return mapped(shards, fine, ("chip", "core"))


def mapped(body, fine, replica):
    tokens, weight, vector = (P(replica, "shard", None), P("shard", None), P("shard"))
    return jax.shard_map(
        body,
        mesh=fine,
        in_specs=(tokens, P(replica, None), tokens, P(replica)) + (weight, vector) * 5,
        out_specs=(tokens, tokens, P(replica, None)) + (weight, vector) * 5,
        check_vma=False,
    )
```

```python
from functools import partial
import math

import jax
import jax.numpy as jnp
from jax import lax
from jax.experimental import pallas as pl
from jax.experimental.pallas import tpu as pltpu
from jax.sharding import PartitionSpec as P

HEADS = 16
HDIM = 72
PADDED = 128
LOG2E = math.log2(math.e)


epsilon = 1e-06


def layer_stats(values):
    centered = values - jnp.mean(values, axis=-1, keepdims=True)
    inverse = lax.rsqrt(jnp.mean(centered * centered, axis=-1, keepdims=True) + epsilon)
    return (centered * inverse, inverse)


def layer_back(normal, inverse, d_normal):
    first_mean = jnp.mean(d_normal, axis=-1, keepdims=True)
    second_mean = jnp.mean(d_normal * normal, axis=-1, keepdims=True)
    return inverse * (d_normal - first_mean - normal * second_mean)


def contract_last(left, right):
    return lax.dot_general(
        left, right, (((1,), (1,)), ((), ())), preferred_element_type=jnp.float32
    )


def forward_product(inputs, whole_pair):
    return (
        jnp.dot(inputs, whole_pair[0], preferred_element_type=jnp.float32),
        whole_pair[1].astype(jnp.float32),
    )


def backward_product(grads, whole_pair):
    return contract_last(grads, whole_pair[0])


def swap_cores(values):
    return lax.ppermute(values, "core", [(0, 1), (1, 0)])


def join_cores(mine, axis):
    theirs = swap_cores(mine)
    first = lax.axis_index("core") == 0
    return jnp.stack(
        [jnp.where(first, mine, theirs), jnp.where(first, theirs, mine)], axis=axis
    )


def gather_rows(weight):
    rows, columns = weight.shape
    cores = lax.axis_size("core")
    part = rows // cores
    mine = lax.dynamic_slice_in_dim(weight, lax.axis_index("core") * part, part, 0)
    pieces = lax.all_gather(mine, "shard", axis=0, tiled=False)
    whole = join_cores(pieces, 1)
    return whole.reshape(rows * lax.axis_size("shard"), columns)


def weight_grad(inputs, grads, after):
    n_shard, n_core = (lax.axis_size("shard"), lax.axis_size("core"))
    terms = lax.dot_general(
        inputs, grads, (((0,), (0,)), ((), ())), preferred_element_type=jnp.float32
    ).astype(jnp.bfloat16)
    rows, columns = terms.shape
    part = rows // (n_shard * n_core)
    terms = terms.reshape(n_shard, n_core, part, columns)
    core = lax.axis_index("core")
    keep = lax.dynamic_index_in_dim(terms, core, 1, keepdims=False)
    send = lax.dynamic_index_in_dim(terms, 1 - core, 1, keepdims=False)
    terms = (keep.astype(jnp.float32) + swap_cores(send).astype(jnp.float32)).astype(jnp.bfloat16)
    terms = lax.psum_scatter(terms, "shard", scatter_dimension=0, tiled=True)
    terms = terms.reshape(part, columns)
    if after is not None:
        terms, _ = lax.optimization_barrier((terms, after))
    total = lax.psum(terms, "chip")
    return total


def finish_grad(total):
    joined = join_cores(total, 0).astype(jnp.float32)
    return joined.reshape(2 * total.shape[0], total.shape[1])


def shards(
    latents,
    conditions,
    cotangent,
    counts,
    w_ada,
    b_ada,
    w_qkv,
    b_qv,
    w_proj,
    b_proj,
    w_fc1,
    b_fc1,
    w_fc2,
    b_fc2,
):
    slots, block, width = latents.shape
    n_rows = slots * block
    scale = 1.0 / math.sqrt(HDIM)
    live = (jnp.arange(slots, dtype=jnp.int32) < counts[0]).astype(jnp.float32)[:, None, None]
    index = lax.axis_index("shard")
    biases = (b_ada, b_qv, b_proj, b_fc1, b_fc2)
    bias_all = lax.all_gather(jnp.concatenate(biases), "shard", axis=0, tiled=False)
    full_bias = []
    start = 0
    for bias in biases:
        size = bias.shape[0]
        full_bias.append(bias_all[:, start : start + size].reshape(-1))
        start += size
    full_qkv = (gather_rows(w_qkv), full_bias[1])
    full_proj = (gather_rows(w_proj), full_bias[2])
    full_fc1 = (gather_rows(w_fc1), full_bias[3])
    full_fc2 = (gather_rows(w_fc2), full_bias[4])
    cond_float = conditions.astype(jnp.float32)
    cond_act = jax.nn.silu(cond_float).astype(jnp.bfloat16)
    ada_rows = w_ada.shape[0]
    ada_length = b_ada.shape[0]
    own_cond = lax.dynamic_slice_in_dim(cond_act, index * ada_rows, ada_rows, 1)
    ada_part = jnp.dot(own_cond, w_ada, preferred_element_type=jnp.float32)
    modul = lax.psum(ada_part, "shard") + full_bias[0].astype(jnp.float32)
    shift_a, scale_a, gate_a, shift_m, scale_m, gate_m = [
        piece[:, None, :] for piece in jnp.split(modul, 6, axis=1)
    ]
    tokens = latents.astype(jnp.float32)
    norm_a, inv_a = layer_stats(tokens)
    normed = (norm_a * (1.0 + scale_a) + shift_a).astype(jnp.bfloat16).reshape(n_rows, width)
    qkv_prod, qv_bias = forward_product(normed, full_qkv)
    query = (
        (qkv_prod[:, :width] + qv_bias[:width])
        .astype(jnp.bfloat16)
        .reshape(slots, block, HEADS, HDIM)
    )
    keys_own = qkv_prod[:, width : 2 * width].astype(jnp.bfloat16).reshape(slots, block, width)
    values_own = (
        (qkv_prod[:, 2 * width :] + qv_bias[width:])
        .astype(jnp.bfloat16)
        .reshape(slots, block, width)
    )
    keys_all, values_all = (
        lax.all_gather(keys_own, "shard", axis=1, tiled=True),
        lax.all_gather(values_own, "shard", axis=1, tiled=True),
    )
    length = keys_all.shape[1]
    keys_h = keys_all.reshape(slots, length, HEADS, HDIM)
    values_h = values_all.reshape(slots, length, HEADS, HDIM)
    scores = (
        jnp.einsum("sqhd,skhd->shqk", query, keys_h, preferred_element_type=jnp.float32) * scale
    )
    top_score = jnp.max(scores, axis=-1, keepdims=True)
    log_total = top_score + jnp.log(jnp.sum(jnp.exp(scores - top_score), axis=-1, keepdims=True))
    probs_low = jnp.exp(scores - log_total).astype(jnp.bfloat16)
    attended = jnp.einsum(
        "shqk,skhd->sqhd", probs_low, values_h, preferred_element_type=jnp.float32
    )
    attended_wide = attended
    attended = attended.astype(jnp.bfloat16).reshape(n_rows, width)
    proj_prod, proj_bias = forward_product(attended, full_proj)
    branch_a = (proj_prod + proj_bias).reshape(slots, block, width)
    resid = tokens + gate_a * branch_a
    norm_m, inv_m = layer_stats(resid)
    mixed = (norm_m * (1.0 + scale_m) + shift_m).astype(jnp.bfloat16).reshape(n_rows, width)
    fc1_prod, fc1_bias = forward_product(mixed, full_fc1)
    activated, gelu_back = jax.vjp(partial(jax.nn.gelu, approximate=True), fc1_prod + fc1_bias)
    hidden = activated.astype(jnp.bfloat16)
    fc2_prod, fc2_bias = forward_product(hidden, full_fc2)
    branch_m = (fc2_prod + fc2_bias).reshape(slots, block, width)
    final = resid + gate_m * branch_m
    output = (final * live).astype(jnp.bfloat16)
    d_out = cotangent.astype(jnp.float32) * live
    d_gate_m = jnp.sum(d_out * branch_m, axis=1)
    d_branch_m = (gate_m * d_out).astype(jnp.bfloat16).reshape(n_rows, width)
    sum_fc2 = weight_grad(hidden, d_branch_m, None)
    bias_fc2 = jnp.sum(d_branch_m, axis=0, dtype=jnp.float32)
    d_hidden = backward_product(d_branch_m, full_fc2)
    d_pre = gelu_back(d_hidden)[0].astype(jnp.bfloat16)
    sum_fc1 = weight_grad(mixed, d_pre, sum_fc2)
    bias_fc1 = jnp.sum(d_pre, axis=0, dtype=jnp.float32)
    d_mixed = backward_product(d_pre, full_fc1).reshape(slots, block, width)
    d_shift_m = jnp.sum(d_mixed, axis=1)
    d_scale_m = jnp.sum(d_mixed * norm_m, axis=1)
    d_resid = d_out + layer_back(norm_m, inv_m, d_mixed * (1.0 + scale_m))
    d_gate_a = jnp.sum(d_resid * branch_a, axis=1)
    d_branch_a = (gate_a * d_resid).astype(jnp.bfloat16).reshape(n_rows, width)
    sum_proj = weight_grad(attended, d_branch_a, sum_fc1)
    bias_proj = jnp.sum(d_branch_a, axis=0, dtype=jnp.float32)
    d_attended = (
        backward_product(d_branch_a, full_proj)
        .astype(jnp.bfloat16)
        .reshape(slots, block, HEADS, HDIM)
    )
    scores = (
        jnp.einsum("sqhd,skhd->shqk", query, keys_h, preferred_element_type=jnp.float32) * scale
    )
    probs = jnp.exp(scores - log_total)
    d_probs = jnp.einsum(
        "sqhd,skhd->shqk", d_attended, values_h, preferred_element_type=jnp.float32
    )
    inner = jnp.sum(d_attended.astype(jnp.float32) * attended_wide, axis=-1)
    inner = jnp.swapaxes(inner, 1, 2)[..., None]
    d_scores = (probs * (d_probs - inner)).astype(jnp.bfloat16)
    d_query = (
        (
            jnp.einsum("shqk,skhd->sqhd", d_scores, keys_h, preferred_element_type=jnp.float32)
            * scale
        )
        .astype(jnp.bfloat16)
        .reshape(n_rows, width)
    )
    key_terms = (
        jnp.einsum("shqk,sqhd->skhd", d_scores, query, preferred_element_type=jnp.float32).reshape(
            slots, length, width
        )
        * scale
    )
    value_terms = jnp.einsum(
        "shqk,sqhd->skhd",
        probs.astype(jnp.bfloat16),
        d_attended,
        preferred_element_type=jnp.float32,
    ).reshape(slots, length, width)
    d_keys, d_values = (
        lax.psum_scatter(
            key_terms.astype(jnp.bfloat16), "shard", scatter_dimension=1, tiled=True
        ).astype(jnp.float32),
        lax.psum_scatter(
            value_terms.astype(jnp.bfloat16), "shard", scatter_dimension=1, tiled=True
        ).astype(jnp.float32),
    )
    d_keys = d_keys.astype(jnp.bfloat16).reshape(n_rows, width)
    d_values = d_values.astype(jnp.bfloat16).reshape(n_rows, width)
    d_qkv = jnp.concatenate([d_query, d_keys, d_values], axis=1)
    qv_terms = jnp.concatenate(
        [jnp.sum(d_query, axis=0, dtype=jnp.float32), jnp.sum(d_values, axis=0, dtype=jnp.float32)]
    )
    sum_qkv = weight_grad(normed, d_qkv, sum_proj)
    d_normed = backward_product(d_qkv, full_qkv).reshape(slots, block, width)
    d_shift_a = jnp.sum(d_normed, axis=1)
    d_scale_a = jnp.sum(d_normed * norm_a, axis=1)
    grad_latents = d_resid + layer_back(norm_a, inv_a, d_normed * (1.0 + scale_a))
    d_modul_part = jnp.concatenate(
        [d_shift_a, d_scale_a, d_gate_a, d_shift_m, d_scale_m, d_gate_m], axis=1
    )
    d_modul = lax.psum(d_modul_part, "shard").astype(jnp.bfloat16)
    cond_all = lax.all_gather(own_cond, ("chip", "core"), axis=0, tiled=True)
    d_modul_all = lax.all_gather(d_modul, ("chip", "core"), axis=0, tiled=True)
    grad_w_ada = lax.dot_general(
        cond_all, d_modul_all, (((0,), (0,)), ((), ())), preferred_element_type=jnp.float32
    )
    grad_b_ada = lax.dynamic_slice_in_dim(
        jnp.sum(d_modul_all, axis=0, dtype=jnp.float32), index * ada_length, ada_length, 0
    )
    d_cond_act = lax.all_gather(contract_last(d_modul, w_ada), "shard", axis=1, tiled=True)
    _, silu_back = jax.vjp(jax.nn.silu, cond_float)
    grad_conditions = silu_back(d_cond_act)[0]
    bias_terms = lax.psum(
        jnp.concatenate([qv_terms, bias_proj, bias_fc1, bias_fc2]), ("chip", "core", "shard")
    )
    bias_grads = []
    start = 0
    for bias in biases[1:]:
        size = bias.shape[0]
        bias_grads.append(
            lax.dynamic_slice_in_dim(bias_terms, start + index * size, size, 0)
        )
        start += size * lax.axis_size("shard")
    return (
        output,
        grad_latents,
        grad_conditions,
        grad_w_ada,
        grad_b_ada,
        finish_grad(sum_qkv),
        bias_grads[0],
        finish_grad(sum_proj),
        bias_grads[1],
        finish_grad(sum_fc1),
        bias_grads[2],
        finish_grad(sum_fc2),
        bias_grads[3],
    )


def contract_first(a,b): return lax.dot_general(a,b,(((0,),(0,)),((),())),preferred_element_type=jnp.float32)

def split_heads(src, dst, first=0):
    rows = src.shape[0]
    for h in range(dst.shape[0]):
        piece = src[:, first + h*HDIM: first + (h+1)*HDIM]
        dst[h] = jnp.concatenate([piece, jnp.zeros((rows, PADDED-HDIM), piece.dtype)], axis=1)

def merge_heads(src, dst, first):
    for h in range(src.shape[0]):
        dst[:, first + h*HDIM: first + (h+1)*HDIM] = src[h][:, :HDIM].astype(dst.dtype)

def attend_body(qkv_ref, lse_ref, qh, kh, vh, oh):
    count = qkv_ref.shape[0]
    heads = qh.shape[0]
    block = count // 2
    scale = LOG2E / math.sqrt(HDIM)
    for t, held in enumerate((qh, kh, vh)):
        split_heads(qkv_ref, held, t * heads * HDIM)

    @pl.loop(0, heads)
    def _(h):
        keys = kh[h]
        values = vh[h]
        for b in range(count // block):
            rows = pl.ds(b * block, block)
            scores = contract_last(keys, qh[h, rows, :])
            top = jnp.max(scores, axis=0, keepdims=True)
            probs = jnp.exp2((scores - top) * scale)
            total = jnp.sum(probs, axis=0, keepdims=True)
            lse_ref[h, :, rows] = top * scale + jnp.log2(total)
            mixed = contract_first(probs.astype(jnp.bfloat16), values)
            oh[h, rows, :] = (mixed * jnp.transpose(1.0 / total)).astype(oh.dtype)


def attend_first_kernel(qkv_ref, out_ref, lse_ref, *held):
    attend_body(qkv_ref, lse_ref, *held)
    merge_heads(held[-1], out_ref, 0)


def attend_second_kernel(qkv_ref, first_ref, out_ref, lse_ref, *held):
    attend_body(qkv_ref, lse_ref, *held)
    out_ref[:, : first_ref.shape[1]] = first_ref[...]
    merge_heads(held[-1], out_ref, first_ref.shape[1])


def attend(qkv, first):
    count, width = qkv.shape[0], qkv.shape[1] // 3
    heads = width // HDIM
    given = [qkv] if first is None else [qkv, first]
    return pl.pallas_call(
        attend_first_kernel if first is None else attend_second_kernel,
        out_shape=(
            jax.ShapeDtypeStruct((count, width * len(given)), jnp.bfloat16),
            jax.ShapeDtypeStruct((heads, 1, count), jnp.float32),
        ),
        in_specs=[pl.BlockSpec(memory_space=pltpu.VMEM)] * len(given),
        out_specs=(pl.BlockSpec(memory_space=pltpu.VMEM),) * 2,
        scratch_shapes=[pltpu.VMEM((heads, count, PADDED), jnp.bfloat16)] * 4,
        compiler_params=pltpu.CompilerParams(vmem_limit_bytes=56 * 2**20),
        cost_estimate=pl.CostEstimate(
            flops=count * width,
            bytes_accessed=count * width,
            transcendentals=0,
        ),
    )(*given)


def attend_back_kernel(
    half, qkv_ref, a_ref, d_ref, lse_ref, out_ref, qh, kh, vh, dh, delta, dqh, dkh, dvh
):
    count = qkv_ref.shape[0]
    heads = qh.shape[0]
    block = count // 2
    root = 1.0 / math.sqrt(HDIM)
    scale = LOG2E * root
    first = half * heads * HDIM
    for t, held in enumerate((qh, kh, vh)):
        split_heads(qkv_ref, held, t * heads * HDIM)
    split_heads(d_ref, dh, first)
    ones = jnp.ones((8, HDIM), jnp.float32)
    for h in range(heads):
        columns = slice(first + h * HDIM, first + (h + 1) * HDIM)
        product = a_ref[:, columns].astype(jnp.float32) * d_ref[:, columns].astype(jnp.float32)
        delta[h] = lax.dot_general(
            ones,
            product,
            (((1,), (1,)), ((), ())),
            preferred_element_type=jnp.float32,
            precision=lax.Precision.HIGHEST,
        )

    @pl.loop(0, heads)
    def _(h):
        query = qh[h]
        grad = dh[h]
        lse = lse_ref[h]
        inner = delta[h, 0:1, :]
        d_query = None
        for b in range(count // block):
            rows = pl.ds(b * block, block)
            keys = kh[h, rows, :]
            scores = contract_last(keys, query)
            probs = jnp.exp2(scores * scale - lse)
            d_probs = contract_last(vh[h, rows, :], grad)
            d_scores = (probs * (d_probs - inner)).astype(jnp.bfloat16)
            dvh[h, rows, :] = jnp.dot(
                probs.astype(jnp.bfloat16), grad, preferred_element_type=jnp.float32
            ).astype(jnp.bfloat16)
            dkh[h, rows, :] = (
                jnp.dot(d_scores, query, preferred_element_type=jnp.float32) * root
            ).astype(jnp.bfloat16)
            part = contract_first(d_scores, keys)
            d_query = part if d_query is None else d_query + part
        dqh[h] = (d_query * root).astype(jnp.bfloat16)

    for t, held in enumerate((dqh, dkh, dvh)):
        merge_heads(held, out_ref, t * heads * HDIM)


def attend_back(qkv, attended, d_attended, log_total, half):
    count, width = qkv.shape[0], qkv.shape[1] // 3
    heads = width // HDIM
    padded = pltpu.VMEM((heads, count, PADDED), jnp.bfloat16)
    return pl.pallas_call(
        partial(attend_back_kernel, half),
        out_shape=jax.ShapeDtypeStruct(qkv.shape, jnp.bfloat16),
        in_specs=[pl.BlockSpec(memory_space=pltpu.VMEM)] * 4,
        out_specs=pl.BlockSpec(memory_space=pltpu.VMEM),
        scratch_shapes=[padded] * 4 + [pltpu.VMEM((heads, 8, count), jnp.float32)] + [padded] * 3,
        compiler_params=pltpu.CompilerParams(vmem_limit_bytes=56 * 2**20),
        cost_estimate=pl.CostEstimate(
            flops=count * width,
            bytes_accessed=count * width,
            transcendentals=0,
        ),
    )(qkv, attended, d_attended, log_total)


def swap_on(values, axis):
    return lax.ppermute(values, axis, [(0, 1), (1, 0)])


def in_order(mine, theirs, axis_name, axis=0):
    first = lax.axis_index(axis_name) == 0
    return jnp.stack(
        [jnp.where(first, mine, theirs), jnp.where(first, theirs, mine)], axis=axis
    )


def pick(values, index, axis):
    return lax.dynamic_index_in_dim(values, index, axis, keepdims=False)


def after(value, *earlier):
    return lax.optimization_barrier((value,) + earlier)[0]


def fetch_start(weight, *earlier):
    part = weight.shape[0] // 4
    x, c = lax.axis_index("x"), lax.axis_index("core")
    mine = lax.dynamic_slice_in_dim(weight, (x * 2 + c) * part, part, 0)
    return swap_on(after(mine, *earlier) if earlier else mine, "shard")


def fetch_rest(mine):
    beside = swap_on(mine, "x")
    return (mine, beside, swap_on(mine, "core"), swap_on(beside, "core"))


def blank_kernel(out_ref):
    pass


def blank(shape, dtype):
    return pl.pallas_call(
        blank_kernel,
        out_shape=jax.ShapeDtypeStruct(shape, dtype),
        out_specs=pl.BlockSpec(memory_space=pl.ANY),
        compiler_params=pltpu.CompilerParams(vmem_limit_bytes=2**20),
    )()


def whole_weight(weight, pieces):
    rows, columns = weight.shape
    part = rows // 4
    s, x, c = lax.axis_index("shard"), lax.axis_index("x"), lax.axis_index("core")
    whole = blank((2 * rows, columns), weight.dtype)
    whole = lax.dynamic_update_slice_in_dim(whole, weight, s * rows, 0)
    base = (1 - s) * rows
    spots = ((x, c), (1 - x, c), (x, 1 - c), (1 - x, 1 - c))
    for piece, (px, pc) in zip(pieces, spots):
        whole = lax.dynamic_update_slice_in_dim(
            whole, piece[:, :columns], base + (px * 2 + pc) * part, 0
        )
    return whole


def split_terms_kernel(core_ref, inputs_ref, grads_ref, keep_ref, send_ref, turned):
    part = keep_ref.shape[2]

    @pl.when(pl.program_id(0) == 0)
    def _():
        turned[...] = inputs_ref[...].T

    terms = jnp.dot(turned[...], grads_ref[...], preferred_element_type=jnp.float32)
    terms = terms.astype(jnp.bfloat16)
    core = core_ref[0]
    for side, other in ((keep_ref, False), (send_ref, True)):
        for c in range(2):
            @pl.when((core != c) if other else (core == c))
            def _():
                for s in range(2):
                    for x in range(2):
                        first = (s * 4 + c * 2 + x) * part
                        side[s, x] = terms[first : first + part]


def split_terms(inputs, grads, columns):
    count, rows = inputs.shape
    width = grads.shape[1]
    part = rows // 8
    core = lax.axis_index("core").astype(jnp.int32).reshape(1)
    out = jax.ShapeDtypeStruct((2, 2, part, width), jnp.bfloat16)
    spec = pl.BlockSpec((2, 2, part, columns), lambda i, core: (0, 0, 0, i))
    keep, send = pl.pallas_call(
        split_terms_kernel,
        out_shape=(out, out),
        grid_spec=pltpu.PrefetchScalarGridSpec(
            num_scalar_prefetch=1,
            grid=(width // columns,),
            in_specs=[
                pl.BlockSpec((count, rows), lambda i, core: (0, 0)),
                pl.BlockSpec((count, columns), lambda i, core: (0, i)),
            ],
            out_specs=(spec, spec),
            scratch_shapes=[pltpu.VMEM((rows, count), jnp.bfloat16)],
        ),
        compiler_params=pltpu.CompilerParams(vmem_limit_bytes=56 * 2**20),
        cost_estimate=pl.CostEstimate(
            flops=count * rows,
            bytes_accessed=count * rows,
            transcendentals=0,
        ),
    )(core, inputs, grads)
    return keep, send


def join_core(pair):
    return add_low(pair[0], swap_on(pair[1], "core"))


def add_low(*terms):
    total = terms[0].astype(jnp.float32)
    for term in terms[1:]:
        total = total + term.astype(jnp.float32)
    return total.astype(jnp.bfloat16)


def split_on(values, axis_name, axis):
    index = lax.axis_index(axis_name)
    return pick(values, index, axis), pick(values, 1 - index, axis)


def keep_and_send(values, axis_name, axis):
    keep, send = split_on(values, axis_name, axis)
    return add_low(keep, swap_on(send, axis_name))


def z_levels():
    return lax.axis_size("z").bit_length() - 1


def z_bit(level):
    return (lax.axis_index("z") >> level) & 1


def swap_z(values, level):
    size = lax.axis_size("z")
    return lax.ppermute(values, "z", [(i, i ^ (1 << level)) for i in range(size)])


def z_order(values, level):
    theirs = swap_z(values, level)
    low = z_bit(level) == 0
    return jnp.stack([jnp.where(low, values, theirs), jnp.where(low, theirs, values)])


def weight_terms(inputs, grads):
    terms = lax.dot_general(
        inputs, grads, (((0,), (0,)), ((), ())), preferred_element_type=jnp.float32
    ).astype(jnp.bfloat16)
    rows, columns = terms.shape
    return terms.reshape(2, 2, 2, rows // 8, columns)


def over_core(terms):
    return keep_and_send(terms, "core", 1)


def over_shard(terms):
    return keep_and_send(terms, "shard", 0)


def qkv_half(weight, half):
    size = weight.shape[-1] // 6
    return jnp.concatenate(
        [weight[..., (2 * t + half) * size : (2 * t + half + 1) * size] for t in range(3)], axis=-1
    )


def over_x(terms):
    return keep_and_send(terms, "x", terms.ndim - 3)


def z_down(terms, level):
    rows, columns = terms.shape
    terms = terms.reshape(2, rows // 2, columns)
    bit = z_bit(level)
    return add_low(pick(terms, bit, 0), swap_z(pick(terms, 1 - bit, 0), level))


def z_up(piece, level):
    theirs = swap_z(piece, level)
    low = z_bit(level) == 0
    return jnp.concatenate(
        [jnp.where(low, piece, theirs), jnp.where(low, theirs, piece)], axis=0
    )


def up_x(piece):
    return in_order(piece, swap_on(piece, "x"), "x")


def up_core(pair):
    whole = in_order(pair, swap_on(pair, "core"), "core")
    return whole.reshape(4 * pair.shape[1], pair.shape[2])


def pair_shards(
    latents,
    conditions,
    cotangent,
    counts,
    w_ada,
    b_ada,
    w_qkv,
    b_qv,
    w_proj,
    b_proj,
    w_fc1,
    b_fc1,
    w_fc2,
    b_fc2,
):
    slots, block, width = latents.shape
    n_rows = slots * block
    s = lax.axis_index("shard")
    live = (s < counts[0]).astype(jnp.float32)

    x, c = lax.axis_index("x"), lax.axis_index("core")
    part = w_qkv.shape[0] // 4
    quarter = lax.dynamic_slice_in_dim(w_qkv, (x * 2 + c) * part, part, 0)
    quarters = [qkv_half(quarter, half) for half in range(2)]
    qkv_mine = [swap_on(quarters[0], "shard"), swap_on(quarters[1], "shard")]
    conditions, b_ada, qkv_mine[0] = lax.optimization_barrier((conditions, b_ada, qkv_mine[0]))
    biases = (b_ada, b_qv, b_proj, b_fc1, b_fc2)
    packed = jnp.concatenate(biases)
    bias_all = in_order(packed, swap_on(packed, "shard"), "shard")
    full_bias = []
    start = 0
    for bias in biases:
        size = bias.shape[0]
        full_bias.append(bias_all[:, start : start + size].reshape(-1).astype(jnp.float32))
        start += size
    ada_bias, qv_bias, proj_bias, fc1_bias, fc2_bias = full_bias
    qkv_bias = jnp.concatenate([qv_bias[:width], jnp.zeros_like(qv_bias[:width]), qv_bias[width:]])
    cond_float = conditions.astype(jnp.float32)
    cond_act = jax.nn.silu(cond_float).astype(jnp.bfloat16)
    ada_rows = w_ada.shape[0]
    own_cond = lax.dynamic_slice_in_dim(cond_act, s * ada_rows, ada_rows, 1)
    ada_part = jnp.dot(own_cond, w_ada, preferred_element_type=jnp.float32)
    modul = pick(ada_part, s, 0) + swap_on(pick(ada_part, 1 - s, 0), "shard") + ada_bias
    shift_a, scale_a, gate_a, shift_m, scale_m, gate_m = [
        piece[None, :] for piece in jnp.split(modul, 6)
    ]
    own_tokens = pick(latents, s, 0)
    far_tokens = swap_on(after(pick(latents, 1 - s, 0), qkv_mine[0]), "shard")
    qkv_pieces = [fetch_rest(mine) for mine in qkv_mine]
    fc1_mine = fetch_start(jnp.concatenate([w_fc1, w_proj], axis=1), far_tokens, qkv_mine[1])
    fc1_pieces = fetch_rest(fc1_mine)
    fc2_mine = fetch_start(w_fc2, fc1_mine)
    fc2_beside = swap_on(fc2_mine, "x")
    fc2_across = swap_on(fc2_mine, "core")
    far_cotangent = swap_on(after(pick(cotangent, 1 - s, 0), fc2_mine), "shard")

    full_qkv = [whole_weight(qkv_half(w_qkv, half), qkv_pieces[half]) for half in range(2)]
    tokens = jnp.concatenate([own_tokens, far_tokens], axis=0).astype(jnp.float32)
    norm_a, inv_a = layer_stats(tokens)
    normed = (norm_a * (1.0 + scale_a) + shift_a).astype(jnp.bfloat16)

    def project(half):
        product = jnp.dot(normed, full_qkv[half], preferred_element_type=jnp.float32)
        return (product + qkv_half(qkv_bias, half)).astype(jnp.bfloat16)

    qkv = [project(0), project(1)]
    first = attend(qkv[0], None)
    qkv[1], fc1_mine, first = lax.optimization_barrier((qkv[1], fc1_mine, first))
    attended, log_second = attend(qkv[1], first[0])
    log_total = [first[1], log_second]
    attended, fc2_mine = lax.optimization_barrier((attended, fc2_mine))
    full_proj = whole_weight(w_proj, [p[:, w_fc1.shape[1]:] for p in fc1_pieces])
    full_fc1 = whole_weight(w_fc1, fc1_pieces)
    branch_a = jnp.dot(attended, full_proj, preferred_element_type=jnp.float32) + proj_bias
    resid = tokens + gate_a * branch_a
    norm_m, inv_m = layer_stats(resid)
    mixed = (norm_m * (1.0 + scale_m) + shift_m).astype(jnp.bfloat16)
    pre = jnp.dot(mixed, full_fc1, preferred_element_type=jnp.float32) + fc1_bias
    activated, gelu_back = jax.vjp(partial(jax.nn.gelu, approximate=True), pre)
    hidden = activated.astype(jnp.bfloat16)
    hidden, fc2_beside, fc2_across = lax.optimization_barrier((hidden, fc2_beside, fc2_across))
    fc2_pieces = (fc2_mine, fc2_beside, fc2_across, swap_on(fc2_beside, "core"))
    full_fc2 = whole_weight(w_fc2, fc2_pieces)
    branch_m = jnp.dot(hidden, full_fc2, preferred_element_type=jnp.float32) + fc2_bias
    branch_m, far_cotangent = lax.optimization_barrier((branch_m, far_cotangent))
    cotangents = jnp.concatenate([pick(cotangent, s, 0), far_cotangent], axis=0)
    out = ((resid + gate_m * branch_m) * live).astype(jnp.bfloat16)
    out, hidden = lax.optimization_barrier((out, hidden))
    out_other = swap_on(out[block:], "shard")

    d_out = cotangents.astype(jnp.float32) * live
    d_gate_m = jnp.sum(d_out * branch_m, axis=0)
    d_branch_m = (gate_m * d_out).astype(jnp.bfloat16)
    sum_fc2 = weight_terms(hidden, d_branch_m)
    bias_fc2 = jnp.sum(d_branch_m, axis=0, dtype=jnp.float32)
    d_branch_m = after(d_branch_m, sum_fc2)
    d_pre = gelu_back(contract_last(d_branch_m, full_fc2))[0].astype(jnp.bfloat16)
    keep_fc2, send_fc2 = split_on(over_core(sum_fc2), "shard", 0)
    d_pre, keep_fc2, send_fc2, out_other = lax.optimization_barrier(
        (d_pre, keep_fc2, send_fc2, out_other)
    )
    came_fc2 = swap_on(send_fc2, "shard")
    sum_fc1 = split_terms(mixed, d_pre, width)
    bias_fc1 = jnp.sum(d_pre, axis=0, dtype=jnp.float32)
    d_pre, sum_fc1 = lax.optimization_barrier((d_pre, sum_fc1))
    d_mixed = contract_last(d_pre, full_fc1)
    keep_fc1, send_fc1 = split_on(join_core(sum_fc1), "x", 1)
    d_mixed, keep_fc1, send_fc1 = lax.optimization_barrier((d_mixed, keep_fc1, send_fc1))
    came_fc1 = swap_on(send_fc1, "x")
    d_shift_m = jnp.sum(d_mixed, axis=0)
    d_scale_m = jnp.sum(d_mixed * norm_m, axis=0)
    d_resid = d_out + layer_back(norm_m, inv_m, d_mixed * (1.0 + scale_m))
    d_gate_a = jnp.sum(d_resid * branch_a, axis=0)
    d_branch_a = (gate_a * d_resid).astype(jnp.bfloat16)
    sum_proj = split_terms(attended, d_branch_a, width)
    bias_proj = jnp.sum(d_branch_a, axis=0, dtype=jnp.float32)
    d_attended = contract_last(d_branch_a, full_proj).astype(jnp.bfloat16)
    sum_proj = join_core(sum_proj)
    sum_fc2 = add_low(keep_fc2, came_fc2)
    d_attended, sum_fc2, sum_proj = lax.optimization_barrier((d_attended, sum_fc2, sum_proj))
    d_first = attend_back(qkv[0], attended, d_attended, log_total[0], 0)
    sum_fc1 = add_low(keep_fc1, came_fc1)
    sum_fc2 = over_x(sum_fc2)
    d_attended, sum_fc1, sum_fc2, d_first = lax.optimization_barrier(
        (d_attended, sum_fc1, sum_fc2, d_first)
    )
    levels = list(range(z_levels()))
    low, high = levels[: len(levels) // 2], levels[len(levels) // 2 :]

    def down(terms, which):
        for level in which:
            terms = z_down(terms, level)
        return terms

    def up(piece, which):
        for level in reversed(which):
            piece = z_up(piece, level)
        return piece

    sum_half = split_terms(normed, d_first, d_first.shape[1])
    sum_fc2 = down(sum_fc2, low)
    d_attended, sum_half, sum_fc2 = lax.optimization_barrier((d_attended, sum_half, sum_fc2))
    d_second = attend_back(qkv[1], attended, d_attended, log_total[1], 1)
    sum_early = jnp.concatenate([sum_proj, join_core(sum_half)], axis=-1)
    sum_fc1 = over_shard(sum_fc1)
    sum_fc2 = down(sum_fc2, high)
    d_second, sum_early, sum_fc2, sum_fc1 = lax.optimization_barrier(
        (d_second, sum_early, sum_fc2, sum_fc1)
    )
    sum_half = split_terms(normed, d_second, d_second.shape[1])
    bias_qv = [jnp.sum(d, axis=0, dtype=jnp.float32) for d in (d_first, d_second)]
    half_width = width // 2
    bias_qv = jnp.concatenate(
        [b[t * half_width : (t + 1) * half_width] for t in (0, 2) for b in bias_qv]
    )
    sum_fc2 = up(sum_fc2, high)
    sum_fc1 = down(sum_fc1, low)
    d_second, sum_half, sum_fc2, sum_fc1 = lax.optimization_barrier(
        (d_second, sum_half, sum_fc2, sum_fc1)
    )
    d_normed = contract_last(d_first, full_qkv[0]) + contract_last(d_second, full_qkv[1])
    keep_late, send_late = split_on(join_core(sum_half), "shard", 0)
    d_normed, keep_late, send_late = lax.optimization_barrier((d_normed, keep_late, send_late))
    came_late = swap_on(send_late, "shard")
    sum_early = over_x(over_shard(sum_early))
    sum_fc2 = up(sum_fc2, low)
    sum_fc1 = down(sum_fc1, high)
    d_shift_a = jnp.sum(d_normed, axis=0)
    d_scale_a = jnp.sum(d_normed * norm_a, axis=0)
    d_modul = jnp.concatenate(
        [d_shift_a, d_scale_a, d_gate_a, d_shift_m, d_scale_m, d_gate_m]
    ).astype(jnp.bfloat16)
    sum_late = add_low(keep_late, came_late)
    output = in_order(out[:block], out_other, "shard")
    d_modul, d_normed, sum_late, sum_early, sum_fc2, sum_fc1 = lax.optimization_barrier(
        (d_modul, d_normed, sum_late, sum_early, sum_fc2, sum_fc1)
    )
    row = jnp.concatenate([d_modul, pick(cond_act, s, 0)])
    terms = [t.reshape(2, -1) for t in (bias_qv, bias_proj, bias_fc1, bias_fc2)]
    terms = jnp.concatenate(terms, axis=1)
    sent = jnp.concatenate([row, pick(terms, 1 - s, 0).astype(jnp.bfloat16)])
    came = swap_on(sent, "shard")
    length = row.shape[0]
    table = in_order(row, came[:length], "shard")
    d_modul_pair = table[:, : d_modul.shape[0]]
    total = pick(terms, s, 0) + came[length:].astype(jnp.float32)

    def grow(table, total, swap):
        both = swap(jnp.concatenate([table.reshape(-1), total.astype(jnp.bfloat16)]))
        size = table.size
        return (
            both[:, :size].reshape(-1, length),
            jnp.sum(both[:, size:].astype(jnp.float32), axis=0),
        )

    sum_late = over_x(sum_late)
    sum_early = down(sum_early, low)
    sum_fc1 = up(sum_fc1, high)
    pair_fc2 = up_x(sum_fc2)
    sum_late, sum_early, sum_fc1, table, total, d_normed = lax.optimization_barrier(
        (sum_late, sum_early, sum_fc1, table, total, d_normed)
    )
    sum_late = down(sum_late, low)
    sum_early = down(sum_early, high)
    sum_fc1 = up(sum_fc1, low)
    grad_tokens = d_resid + layer_back(norm_a, inv_a, d_normed * (1.0 + scale_a))
    table, total = grow(table, total, lambda v: in_order(v, swap_on(v, "core"), "core"))
    sum_late, sum_early, sum_fc1, table, total, grad_tokens = lax.optimization_barrier(
        (sum_late, sum_early, sum_fc1, table, total, grad_tokens)
    )
    sum_late = down(sum_late, high)
    sum_early = up(sum_early, high)
    far_grad = swap_on(grad_tokens[block:].astype(jnp.bfloat16), "shard")
    pair_fc1 = up_x(sum_fc1)
    table, total = grow(table, total, lambda v: in_order(v, swap_on(v, "x"), "x"))
    sum_late, sum_early, table, total = lax.optimization_barrier(
        (sum_late, sum_early, table, total)
    )
    sum_late = up(sum_late, high)
    sum_early = up(sum_early, low)
    grad_fc2 = up_core(pair_fc2).astype(jnp.float32)
    for level in low:
        table, total = grow(table, total, lambda v: z_order(v, level))
    sum_late, sum_early, far_grad, table, total, grad_fc2 = lax.optimization_barrier(
        (sum_late, sum_early, far_grad, table, total, grad_fc2)
    )
    sum_late = up(sum_late, low)
    pair_early = up_x(sum_early)
    for level in high:
        table, total = grow(table, total, lambda v: z_order(v, level))
    grad_fc1 = up_core(pair_fc1).astype(jnp.float32)
    sum_late, table, total, grad_fc1 = lax.optimization_barrier(
        (sum_late, table, total, grad_fc1)
    )
    pair_late = up_x(sum_late)
    grad_latents = in_order(grad_tokens[:block], far_grad.astype(jnp.float32), "shard")
    halves = (pair_early[..., width:], pair_late)
    pair_qkv = jnp.concatenate(
        [
            piece[..., t * half_width : (t + 1) * half_width]
            for t in range(3)
            for piece in halves
        ],
        axis=-1,
    )
    grad_proj = up_core(pair_early[..., :width]).astype(jnp.float32)
    grad_qkv = up_core(pair_qkv).astype(jnp.float32)

    d_modul_all, cond_all = table[:, : d_modul.shape[0]], table[:, d_modul.shape[0] :]
    cond_all = lax.dynamic_slice_in_dim(cond_all, s * ada_rows, ada_rows, 1)
    grad_w_ada = lax.dot_general(
        cond_all, d_modul_all, (((0,), (0,)), ((), ())), preferred_element_type=jnp.float32
    )
    ada_length = b_ada.shape[0]
    grad_b_ada = lax.dynamic_slice_in_dim(
        jnp.sum(d_modul_all, axis=0, dtype=jnp.float32), s * ada_length, ada_length, 0
    )
    d_cond = contract_last(d_modul_pair, w_ada)
    d_cond = in_order(d_cond, swap_on(d_cond, "shard"), "shard")
    d_cond_act = jnp.moveaxis(d_cond, 0, 1).reshape(slots, width)
    _, silu_back = jax.vjp(jax.nn.silu, cond_float)
    grad_conditions = silu_back(d_cond_act)[0]
    bias_grads = []
    start = 0
    for bias in biases[1:]:
        size = bias.shape[0]
        bias_grads.append(total[start : start + size])
        start += size
    return (
        output,
        grad_latents,
        grad_conditions,
        grad_w_ada,
        grad_b_ada,
        grad_qkv,
        bias_grads[0],
        grad_proj,
        bias_grads[1],
        grad_fc1,
        bias_grads[2],
        grad_fc2,
        bias_grads[3],
    )


def solution(mesh):
    n_z = mesh.shape["replica"] // 4
    if mesh.shape["shard"] == 2 and n_z & (n_z - 1) == 0 and mesh.shape["replica"] % 4 == 0:
        return pair_solution(mesh)
    return wide_solution(mesh)


def pair_solution(mesh):
    names = mesh.axis_names
    n_replica, n_shard = (mesh.shape["replica"], mesh.shape["shard"])
    devices = mesh.devices.transpose(names.index("replica"), names.index("shard"))
    fine = jax.sharding.Mesh(
        devices.reshape(n_replica // 4, 2, 2, n_shard), ("z", "x", "core", "shard")
    )
    return mapped(pair_shards, fine, ("z", "x", "core"))


def wide_solution(mesh):
    names = mesh.axis_names
    n_replica, n_shard = (mesh.shape["replica"], mesh.shape["shard"])
    devices = mesh.devices.transpose(names.index("replica"), names.index("shard"))
    fine = jax.sharding.Mesh(
        devices.reshape(n_replica // 2, 2, n_shard), ("chip", "core", "shard")
    )
    return mapped(shards, fine, ("chip", "core"))


def mapped(body, fine, replica):
    tokens, weight, vector = (P(replica, "shard", None), P("shard", None), P("shard"))
    return jax.shard_map(
        body,
        mesh=fine,
        in_specs=(tokens, P(replica, None), tokens, P(replica)) + (weight, vector) * 5,
        out_specs=(tokens, tokens, P(replica, None)) + (weight, vector) * 5,
        check_vma=False,
    )
```

```python
from functools import partial
import math

import jax
import jax.numpy as jnp
from jax import lax
from jax.experimental import pallas as pl
from jax.experimental.pallas import tpu as pltpu
from jax.sharding import PartitionSpec as P

HEADS = 16
HDIM = 72
PADDED = 128
LOG2E = math.log2(math.e)


epsilon = 1e-06


def layer_stats(values):
    centered = values - jnp.mean(values, axis=-1, keepdims=True)
    inverse = lax.rsqrt(jnp.mean(centered * centered, axis=-1, keepdims=True) + epsilon)
    return (centered * inverse, inverse)


def layer_back(normal, inverse, d_normal):
    first_mean = jnp.mean(d_normal, axis=-1, keepdims=True)
    second_mean = jnp.mean(d_normal * normal, axis=-1, keepdims=True)
    return inverse * (d_normal - first_mean - normal * second_mean)


def contract_last(left, right):
    return lax.dot_general(
        left, right, (((1,), (1,)), ((), ())), preferred_element_type=jnp.float32
    )


def forward_product(inputs, whole_pair):
    return (
        jnp.dot(inputs, whole_pair[0], preferred_element_type=jnp.float32),
        whole_pair[1].astype(jnp.float32),
    )


def backward_product(grads, whole_pair):
    return contract_last(grads, whole_pair[0])


def swap_cores(values):
    return lax.ppermute(values, "core", [(0, 1), (1, 0)])


def join_cores(mine, axis):
    theirs = swap_cores(mine)
    first = lax.axis_index("core") == 0
    return jnp.stack(
        [jnp.where(first, mine, theirs), jnp.where(first, theirs, mine)], axis=axis
    )


def gather_rows(weight):
    rows, columns = weight.shape
    cores = lax.axis_size("core")
    part = rows // cores
    mine = lax.dynamic_slice_in_dim(weight, lax.axis_index("core") * part, part, 0)
    pieces = lax.all_gather(mine, "shard", axis=0, tiled=False)
    whole = join_cores(pieces, 1)
    return whole.reshape(rows * lax.axis_size("shard"), columns)


def weight_grad(inputs, grads, after):
    n_shard, n_core = (lax.axis_size("shard"), lax.axis_size("core"))
    terms = lax.dot_general(
        inputs, grads, (((0,), (0,)), ((), ())), preferred_element_type=jnp.float32
    ).astype(jnp.bfloat16)
    rows, columns = terms.shape
    part = rows // (n_shard * n_core)
    terms = terms.reshape(n_shard, n_core, part, columns)
    core = lax.axis_index("core")
    keep = lax.dynamic_index_in_dim(terms, core, 1, keepdims=False)
    send = lax.dynamic_index_in_dim(terms, 1 - core, 1, keepdims=False)
    terms = (keep.astype(jnp.float32) + swap_cores(send).astype(jnp.float32)).astype(jnp.bfloat16)
    terms = lax.psum_scatter(terms, "shard", scatter_dimension=0, tiled=True)
    terms = terms.reshape(part, columns)
    if after is not None:
        terms, _ = lax.optimization_barrier((terms, after))
    total = lax.psum(terms, "chip")
    return total


def finish_grad(total):
    joined = join_cores(total, 0).astype(jnp.float32)
    return joined.reshape(2 * total.shape[0], total.shape[1])


def shards(
    latents,
    conditions,
    cotangent,
    counts,
    w_ada,
    b_ada,
    w_qkv,
    b_qv,
    w_proj,
    b_proj,
    w_fc1,
    b_fc1,
    w_fc2,
    b_fc2,
):
    slots, block, width = latents.shape
    n_rows = slots * block
    scale = 1.0 / math.sqrt(HDIM)
    live = (jnp.arange(slots, dtype=jnp.int32) < counts[0]).astype(jnp.float32)[:, None, None]
    index = lax.axis_index("shard")
    biases = (b_ada, b_qv, b_proj, b_fc1, b_fc2)
    bias_all = lax.all_gather(jnp.concatenate(biases), "shard", axis=0, tiled=False)
    full_bias = []
    start = 0
    for bias in biases:
        size = bias.shape[0]
        full_bias.append(bias_all[:, start : start + size].reshape(-1))
        start += size
    full_qkv = (gather_rows(w_qkv), full_bias[1])
    full_proj = (gather_rows(w_proj), full_bias[2])
    full_fc1 = (gather_rows(w_fc1), full_bias[3])
    full_fc2 = (gather_rows(w_fc2), full_bias[4])
    cond_float = conditions.astype(jnp.float32)
    cond_act = jax.nn.silu(cond_float).astype(jnp.bfloat16)
    ada_rows = w_ada.shape[0]
    ada_length = b_ada.shape[0]
    own_cond = lax.dynamic_slice_in_dim(cond_act, index * ada_rows, ada_rows, 1)
    ada_part = jnp.dot(own_cond, w_ada, preferred_element_type=jnp.float32)
    modul = lax.psum(ada_part, "shard") + full_bias[0].astype(jnp.float32)
    shift_a, scale_a, gate_a, shift_m, scale_m, gate_m = [
        piece[:, None, :] for piece in jnp.split(modul, 6, axis=1)
    ]
    tokens = latents.astype(jnp.float32)
    norm_a, inv_a = layer_stats(tokens)
    normed = (norm_a * (1.0 + scale_a) + shift_a).astype(jnp.bfloat16).reshape(n_rows, width)
    qkv_prod, qv_bias = forward_product(normed, full_qkv)
    query = (
        (qkv_prod[:, :width] + qv_bias[:width])
        .astype(jnp.bfloat16)
        .reshape(slots, block, HEADS, HDIM)
    )
    keys_own = qkv_prod[:, width : 2 * width].astype(jnp.bfloat16).reshape(slots, block, width)
    values_own = (
        (qkv_prod[:, 2 * width :] + qv_bias[width:])
        .astype(jnp.bfloat16)
        .reshape(slots, block, width)
    )
    keys_all, values_all = (
        lax.all_gather(keys_own, "shard", axis=1, tiled=True),
        lax.all_gather(values_own, "shard", axis=1, tiled=True),
    )
    length = keys_all.shape[1]
    keys_h = keys_all.reshape(slots, length, HEADS, HDIM)
    values_h = values_all.reshape(slots, length, HEADS, HDIM)
    scores = (
        jnp.einsum("sqhd,skhd->shqk", query, keys_h, preferred_element_type=jnp.float32) * scale
    )
    top_score = jnp.max(scores, axis=-1, keepdims=True)
    log_total = top_score + jnp.log(jnp.sum(jnp.exp(scores - top_score), axis=-1, keepdims=True))
    probs_low = jnp.exp(scores - log_total).astype(jnp.bfloat16)
    attended = jnp.einsum(
        "shqk,skhd->sqhd", probs_low, values_h, preferred_element_type=jnp.float32
    )
    attended_wide = attended
    attended = attended.astype(jnp.bfloat16).reshape(n_rows, width)
    proj_prod, proj_bias = forward_product(attended, full_proj)
    branch_a = (proj_prod + proj_bias).reshape(slots, block, width)
    resid = tokens + gate_a * branch_a
    norm_m, inv_m = layer_stats(resid)
    mixed = (norm_m * (1.0 + scale_m) + shift_m).astype(jnp.bfloat16).reshape(n_rows, width)
    fc1_prod, fc1_bias = forward_product(mixed, full_fc1)
    activated, gelu_back = jax.vjp(partial(jax.nn.gelu, approximate=True), fc1_prod + fc1_bias)
    hidden = activated.astype(jnp.bfloat16)
    fc2_prod, fc2_bias = forward_product(hidden, full_fc2)
    branch_m = (fc2_prod + fc2_bias).reshape(slots, block, width)
    final = resid + gate_m * branch_m
    output = (final * live).astype(jnp.bfloat16)
    d_out = cotangent.astype(jnp.float32) * live
    d_gate_m = jnp.sum(d_out * branch_m, axis=1)
    d_branch_m = (gate_m * d_out).astype(jnp.bfloat16).reshape(n_rows, width)
    sum_fc2 = weight_grad(hidden, d_branch_m, None)
    bias_fc2 = jnp.sum(d_branch_m, axis=0, dtype=jnp.float32)
    d_hidden = backward_product(d_branch_m, full_fc2)
    d_pre = gelu_back(d_hidden)[0].astype(jnp.bfloat16)
    sum_fc1 = weight_grad(mixed, d_pre, sum_fc2)
    bias_fc1 = jnp.sum(d_pre, axis=0, dtype=jnp.float32)
    d_mixed = backward_product(d_pre, full_fc1).reshape(slots, block, width)
    d_shift_m = jnp.sum(d_mixed, axis=1)
    d_scale_m = jnp.sum(d_mixed * norm_m, axis=1)
    d_resid = d_out + layer_back(norm_m, inv_m, d_mixed * (1.0 + scale_m))
    d_gate_a = jnp.sum(d_resid * branch_a, axis=1)
    d_branch_a = (gate_a * d_resid).astype(jnp.bfloat16).reshape(n_rows, width)
    sum_proj = weight_grad(attended, d_branch_a, sum_fc1)
    bias_proj = jnp.sum(d_branch_a, axis=0, dtype=jnp.float32)
    d_attended = (
        backward_product(d_branch_a, full_proj)
        .astype(jnp.bfloat16)
        .reshape(slots, block, HEADS, HDIM)
    )
    scores = (
        jnp.einsum("sqhd,skhd->shqk", query, keys_h, preferred_element_type=jnp.float32) * scale
    )
    probs = jnp.exp(scores - log_total)
    d_probs = jnp.einsum(
        "sqhd,skhd->shqk", d_attended, values_h, preferred_element_type=jnp.float32
    )
    inner = jnp.sum(d_attended.astype(jnp.float32) * attended_wide, axis=-1)
    inner = jnp.swapaxes(inner, 1, 2)[..., None]
    d_scores = (probs * (d_probs - inner)).astype(jnp.bfloat16)
    d_query = (
        (
            jnp.einsum("shqk,skhd->sqhd", d_scores, keys_h, preferred_element_type=jnp.float32)
            * scale
        )
        .astype(jnp.bfloat16)
        .reshape(n_rows, width)
    )
    key_terms = (
        jnp.einsum("shqk,sqhd->skhd", d_scores, query, preferred_element_type=jnp.float32).reshape(
            slots, length, width
        )
        * scale
    )
    value_terms = jnp.einsum(
        "shqk,sqhd->skhd",
        probs.astype(jnp.bfloat16),
        d_attended,
        preferred_element_type=jnp.float32,
    ).reshape(slots, length, width)
    d_keys, d_values = (
        lax.psum_scatter(
            key_terms.astype(jnp.bfloat16), "shard", scatter_dimension=1, tiled=True
        ).astype(jnp.float32),
        lax.psum_scatter(
            value_terms.astype(jnp.bfloat16), "shard", scatter_dimension=1, tiled=True
        ).astype(jnp.float32),
    )
    d_keys = d_keys.astype(jnp.bfloat16).reshape(n_rows, width)
    d_values = d_values.astype(jnp.bfloat16).reshape(n_rows, width)
    d_qkv = jnp.concatenate([d_query, d_keys, d_values], axis=1)
    qv_terms = jnp.concatenate(
        [jnp.sum(d_query, axis=0, dtype=jnp.float32), jnp.sum(d_values, axis=0, dtype=jnp.float32)]
    )
    sum_qkv = weight_grad(normed, d_qkv, sum_proj)
    d_normed = backward_product(d_qkv, full_qkv).reshape(slots, block, width)
    d_shift_a = jnp.sum(d_normed, axis=1)
    d_scale_a = jnp.sum(d_normed * norm_a, axis=1)
    grad_latents = d_resid + layer_back(norm_a, inv_a, d_normed * (1.0 + scale_a))
    d_modul_part = jnp.concatenate(
        [d_shift_a, d_scale_a, d_gate_a, d_shift_m, d_scale_m, d_gate_m], axis=1
    )
    d_modul = lax.psum(d_modul_part, "shard").astype(jnp.bfloat16)
    cond_all = lax.all_gather(own_cond, ("chip", "core"), axis=0, tiled=True)
    d_modul_all = lax.all_gather(d_modul, ("chip", "core"), axis=0, tiled=True)
    grad_w_ada = lax.dot_general(
        cond_all, d_modul_all, (((0,), (0,)), ((), ())), preferred_element_type=jnp.float32
    )
    grad_b_ada = lax.dynamic_slice_in_dim(
        jnp.sum(d_modul_all, axis=0, dtype=jnp.float32), index * ada_length, ada_length, 0
    )
    d_cond_act = lax.all_gather(contract_last(d_modul, w_ada), "shard", axis=1, tiled=True)
    _, silu_back = jax.vjp(jax.nn.silu, cond_float)
    grad_conditions = silu_back(d_cond_act)[0]
    bias_terms = lax.psum(
        jnp.concatenate([qv_terms, bias_proj, bias_fc1, bias_fc2]), ("chip", "core", "shard")
    )
    bias_grads = []
    start = 0
    for bias in biases[1:]:
        size = bias.shape[0]
        bias_grads.append(
            lax.dynamic_slice_in_dim(bias_terms, start + index * size, size, 0)
        )
        start += size * lax.axis_size("shard")
    return (
        output,
        grad_latents,
        grad_conditions,
        grad_w_ada,
        grad_b_ada,
        finish_grad(sum_qkv),
        bias_grads[0],
        finish_grad(sum_proj),
        bias_grads[1],
        finish_grad(sum_fc1),
        bias_grads[2],
        finish_grad(sum_fc2),
        bias_grads[3],
    )


def contract_first(a,b): return lax.dot_general(a,b,(((0,),(0,)),((),())),preferred_element_type=jnp.float32)

def split_heads(src, dst, first=0):
    rows = src.shape[0]
    for h in range(dst.shape[0]):
        piece = src[:, first + h*HDIM: first + (h+1)*HDIM]
        dst[h] = jnp.concatenate([piece, jnp.zeros((rows, PADDED-HDIM), piece.dtype)], axis=1)

def merge_heads(src, dst, first):
    for h in range(src.shape[0]):
        dst[:, first + h*HDIM: first + (h+1)*HDIM] = src[h][:, :HDIM].astype(dst.dtype)

def attend_body(qkv_ref, lse_ref, qh, kh, vh, oh):
    count = qkv_ref.shape[0]
    heads = qh.shape[0]
    block = count // 2
    scale = LOG2E / math.sqrt(HDIM)
    for t, held in enumerate((qh, kh, vh)):
        split_heads(qkv_ref, held, t * heads * HDIM)

    @pl.loop(0, heads)
    def _(h):
        keys = kh[h]
        values = vh[h]
        for b in range(count // block):
            rows = pl.ds(b * block, block)
            scores = contract_last(keys, qh[h, rows, :])
            top = jnp.max(scores, axis=0, keepdims=True)
            probs = jnp.exp2((scores - top) * scale)
            total = jnp.sum(probs, axis=0, keepdims=True)
            lse_ref[h, :, rows] = top * scale + jnp.log2(total)
            mixed = contract_first(probs.astype(jnp.bfloat16), values)
            oh[h, rows, :] = (mixed * jnp.transpose(1.0 / total)).astype(oh.dtype)


def attend_first_kernel(qkv_ref, out_ref, lse_ref, *held):
    attend_body(qkv_ref, lse_ref, *held)
    merge_heads(held[-1], out_ref, 0)


def attend_second_kernel(qkv_ref, first_ref, out_ref, lse_ref, *held):
    attend_body(qkv_ref, lse_ref, *held)
    out_ref[:, : first_ref.shape[1]] = first_ref[...]
    merge_heads(held[-1], out_ref, first_ref.shape[1])


def attend(qkv, first):
    count, width = qkv.shape[0], qkv.shape[1] // 3
    heads = width // HDIM
    given = [qkv] if first is None else [qkv, first]
    return pl.pallas_call(
        attend_first_kernel if first is None else attend_second_kernel,
        out_shape=(
            jax.ShapeDtypeStruct((count, width * len(given)), jnp.bfloat16),
            jax.ShapeDtypeStruct((heads, 1, count), jnp.float32),
        ),
        in_specs=[pl.BlockSpec(memory_space=pltpu.VMEM)] * len(given),
        out_specs=(pl.BlockSpec(memory_space=pltpu.VMEM),) * 2,
        scratch_shapes=[pltpu.VMEM((heads, count, PADDED), jnp.bfloat16)] * 4,
        compiler_params=pltpu.CompilerParams(vmem_limit_bytes=56 * 2**20),
        cost_estimate=pl.CostEstimate(
            flops=count * width,
            bytes_accessed=count * width,
            transcendentals=0,
        ),
    )(*given)


def attend_back_kernel(
    half, qkv_ref, a_ref, d_ref, lse_ref, out_ref, qh, kh, vh, dh, delta, dqh, dkh, dvh
):
    count = qkv_ref.shape[0]
    heads = qh.shape[0]
    block = count // 2
    root = 1.0 / math.sqrt(HDIM)
    scale = LOG2E * root
    first = half * heads * HDIM
    for t, held in enumerate((qh, kh, vh)):
        split_heads(qkv_ref, held, t * heads * HDIM)
    split_heads(d_ref, dh, first)
    ones = jnp.ones((8, HDIM), jnp.float32)
    for h in range(heads):
        columns = slice(first + h * HDIM, first + (h + 1) * HDIM)
        product = a_ref[:, columns].astype(jnp.float32) * d_ref[:, columns].astype(jnp.float32)
        delta[h] = lax.dot_general(
            ones,
            product,
            (((1,), (1,)), ((), ())),
            preferred_element_type=jnp.float32,
            precision=lax.Precision.HIGHEST,
        )

    @pl.loop(0, heads)
    def _(h):
        query = qh[h]
        grad = dh[h]
        lse = lse_ref[h]
        inner = delta[h, 0:1, :]
        d_query = None
        for b in range(count // block):
            rows = pl.ds(b * block, block)
            keys = kh[h, rows, :]
            scores = contract_last(keys, query)
            probs = jnp.exp2(scores * scale - lse)
            d_probs = contract_last(vh[h, rows, :], grad)
            d_scores = (probs * (d_probs - inner)).astype(jnp.bfloat16)
            dvh[h, rows, :] = jnp.dot(
                probs.astype(jnp.bfloat16), grad, preferred_element_type=jnp.float32
            ).astype(jnp.bfloat16)
            dkh[h, rows, :] = (
                jnp.dot(d_scores, query, preferred_element_type=jnp.float32) * root
            ).astype(jnp.bfloat16)
            part = contract_first(d_scores, keys)
            d_query = part if d_query is None else d_query + part
        dqh[h] = (d_query * root).astype(jnp.bfloat16)

    for t, held in enumerate((dqh, dkh, dvh)):
        merge_heads(held, out_ref, t * heads * HDIM)


def attend_back(qkv, attended, d_attended, log_total, half):
    count, width = qkv.shape[0], qkv.shape[1] // 3
    heads = width // HDIM
    padded = pltpu.VMEM((heads, count, PADDED), jnp.bfloat16)
    return pl.pallas_call(
        partial(attend_back_kernel, half),
        out_shape=jax.ShapeDtypeStruct(qkv.shape, jnp.bfloat16),
        in_specs=[pl.BlockSpec(memory_space=pltpu.VMEM)] * 4,
        out_specs=pl.BlockSpec(memory_space=pltpu.VMEM),
        scratch_shapes=[padded] * 4 + [pltpu.VMEM((heads, 8, count), jnp.float32)] + [padded] * 3,
        compiler_params=pltpu.CompilerParams(vmem_limit_bytes=56 * 2**20),
        cost_estimate=pl.CostEstimate(
            flops=count * width,
            bytes_accessed=count * width,
            transcendentals=0,
        ),
    )(qkv, attended, d_attended, log_total)


def swap_on(values, axis):
    return lax.ppermute(values, axis, [(0, 1), (1, 0)])


def in_order(mine, theirs, axis_name, axis=0):
    first = lax.axis_index(axis_name) == 0
    return jnp.stack(
        [jnp.where(first, mine, theirs), jnp.where(first, theirs, mine)], axis=axis
    )


def pick(values, index, axis):
    return lax.dynamic_index_in_dim(values, index, axis, keepdims=False)


def after(value, *earlier):
    return lax.optimization_barrier((value,) + earlier)[0]


def fetch_start(weight, *earlier):
    part = weight.shape[0] // 4
    x, c = lax.axis_index("x"), lax.axis_index("core")
    mine = lax.dynamic_slice_in_dim(weight, (x * 2 + c) * part, part, 0)
    return swap_on(after(mine, *earlier) if earlier else mine, "shard")


def fetch_rest(mine):
    beside = swap_on(mine, "x")
    return (mine, beside, swap_on(mine, "core"), swap_on(beside, "core"))


def blank_kernel(out_ref):
    pass


def blank(shape, dtype):
    return pl.pallas_call(
        blank_kernel,
        out_shape=jax.ShapeDtypeStruct(shape, dtype),
        out_specs=pl.BlockSpec(memory_space=pl.ANY),
        compiler_params=pltpu.CompilerParams(vmem_limit_bytes=2**20),
    )()


def whole_weight(weight, pieces):
    rows, columns = weight.shape
    part = rows // 4
    s, x, c = lax.axis_index("shard"), lax.axis_index("x"), lax.axis_index("core")
    whole = blank((2 * rows, columns), weight.dtype)
    whole = lax.dynamic_update_slice_in_dim(whole, weight, s * rows, 0)
    base = (1 - s) * rows
    spots = ((x, c), (1 - x, c), (x, 1 - c), (1 - x, 1 - c))
    for piece, (px, pc) in zip(pieces, spots):
        whole = lax.dynamic_update_slice_in_dim(
            whole, piece[:, :columns], base + (px * 2 + pc) * part, 0
        )
    return whole


def split_terms_kernel(core_ref, inputs_ref, grads_ref, keep_ref, send_ref, turned):
    part = keep_ref.shape[2]

    @pl.when(pl.program_id(0) == 0)
    def _():
        turned[...] = inputs_ref[...].T

    terms = jnp.dot(turned[...], grads_ref[...], preferred_element_type=jnp.float32)
    terms = terms.astype(jnp.bfloat16)
    core = core_ref[0]
    for side, other in ((keep_ref, False), (send_ref, True)):
        for c in range(2):
            @pl.when((core != c) if other else (core == c))
            def _():
                for s in range(2):
                    for x in range(2):
                        first = (s * 4 + c * 2 + x) * part
                        side[s, x] = terms[first : first + part]


def split_terms(inputs, grads, columns):
    count, rows = inputs.shape
    width = grads.shape[1]
    part = rows // 8
    core = lax.axis_index("core").astype(jnp.int32).reshape(1)
    out = jax.ShapeDtypeStruct((2, 2, part, width), jnp.bfloat16)
    spec = pl.BlockSpec((2, 2, part, columns), lambda i, core: (0, 0, 0, i))
    keep, send = pl.pallas_call(
        split_terms_kernel,
        out_shape=(out, out),
        grid_spec=pltpu.PrefetchScalarGridSpec(
            num_scalar_prefetch=1,
            grid=(width // columns,),
            in_specs=[
                pl.BlockSpec((count, rows), lambda i, core: (0, 0)),
                pl.BlockSpec((count, columns), lambda i, core: (0, i)),
            ],
            out_specs=(spec, spec),
            scratch_shapes=[pltpu.VMEM((rows, count), jnp.bfloat16)],
        ),
        compiler_params=pltpu.CompilerParams(vmem_limit_bytes=56 * 2**20),
        cost_estimate=pl.CostEstimate(
            flops=count * rows,
            bytes_accessed=count * rows,
            transcendentals=0,
        ),
    )(core, inputs, grads)
    return keep, send


def join_core(pair):
    return add_low(pair[0], swap_on(pair[1], "core"))


def add_low(*terms):
    total = terms[0].astype(jnp.float32)
    for term in terms[1:]:
        total = total + term.astype(jnp.float32)
    return total.astype(jnp.bfloat16)


def split_on(values, axis_name, axis):
    index = lax.axis_index(axis_name)
    return pick(values, index, axis), pick(values, 1 - index, axis)


def keep_and_send(values, axis_name, axis):
    keep, send = split_on(values, axis_name, axis)
    return add_low(keep, swap_on(send, axis_name))


def z_levels():
    return lax.axis_size("z").bit_length() - 1


def z_bit(level):
    return (lax.axis_index("z") >> level) & 1


def swap_z(values, level):
    size = lax.axis_size("z")
    return lax.ppermute(values, "z", [(i, i ^ (1 << level)) for i in range(size)])


def z_order(values, level):
    theirs = swap_z(values, level)
    low = z_bit(level) == 0
    return jnp.stack([jnp.where(low, values, theirs), jnp.where(low, theirs, values)])


def weight_terms(inputs, grads):
    terms = lax.dot_general(
        inputs, grads, (((0,), (0,)), ((), ())), preferred_element_type=jnp.float32
    ).astype(jnp.bfloat16)
    rows, columns = terms.shape
    return terms.reshape(2, 2, 2, rows // 8, columns)


def over_core(terms):
    return keep_and_send(terms, "core", 1)


def over_shard(terms):
    return keep_and_send(terms, "shard", 0)


def qkv_half(weight, half):
    size = weight.shape[-1] // 6
    return jnp.concatenate(
        [weight[..., (2 * t + half) * size : (2 * t + half + 1) * size] for t in range(3)], axis=-1
    )


def over_x(terms):
    return keep_and_send(terms, "x", terms.ndim - 3)


def z_down(terms, level):
    rows, columns = terms.shape
    terms = terms.reshape(2, rows // 2, columns)
    bit = z_bit(level)
    return add_low(pick(terms, bit, 0), swap_z(pick(terms, 1 - bit, 0), level))


def z_up(piece, level):
    theirs = swap_z(piece, level)
    low = z_bit(level) == 0
    return jnp.concatenate(
        [jnp.where(low, piece, theirs), jnp.where(low, theirs, piece)], axis=0
    )


def up_x(piece):
    return in_order(piece, swap_on(piece, "x"), "x")


def up_core(pair):
    whole = in_order(pair, swap_on(pair, "core"), "core")
    return whole.reshape(4 * pair.shape[1], pair.shape[2])


def pair_shards(
    latents,
    conditions,
    cotangent,
    counts,
    w_ada,
    b_ada,
    w_qkv,
    b_qv,
    w_proj,
    b_proj,
    w_fc1,
    b_fc1,
    w_fc2,
    b_fc2,
):
    slots, block, width = latents.shape
    n_rows = slots * block
    s = lax.axis_index("shard")
    live = (s < counts[0]).astype(jnp.float32)

    x, c = lax.axis_index("x"), lax.axis_index("core")
    part = w_qkv.shape[0] // 4
    quarter = lax.dynamic_slice_in_dim(w_qkv, (x * 2 + c) * part, part, 0)
    quarters = [qkv_half(quarter, half) for half in range(2)]
    qkv_mine = [swap_on(quarters[0], "shard"), swap_on(quarters[1], "shard")]
    conditions, b_ada, w_fc2, w_fc1, w_qkv, latents, qkv_mine[0] = lax.optimization_barrier(
        (conditions, b_ada, w_fc2, w_fc1, w_qkv, latents, qkv_mine[0])
    )
    biases = (b_ada, b_qv, b_proj, b_fc1, b_fc2)
    packed = jnp.concatenate(biases)
    bias_all = in_order(packed, swap_on(packed, "shard"), "shard")
    full_bias = []
    start = 0
    for bias in biases:
        size = bias.shape[0]
        full_bias.append(bias_all[:, start : start + size].reshape(-1).astype(jnp.float32))
        start += size
    ada_bias, qv_bias, proj_bias, fc1_bias, fc2_bias = full_bias
    qkv_bias = jnp.concatenate([qv_bias[:width], jnp.zeros_like(qv_bias[:width]), qv_bias[width:]])
    cond_float = conditions.astype(jnp.float32)
    cond_act = jax.nn.silu(cond_float).astype(jnp.bfloat16)
    ada_rows = w_ada.shape[0]
    own_cond = lax.dynamic_slice_in_dim(cond_act, s * ada_rows, ada_rows, 1)
    ada_part = jnp.dot(own_cond, w_ada, preferred_element_type=jnp.float32)
    modul = pick(ada_part, s, 0) + swap_on(pick(ada_part, 1 - s, 0), "shard") + ada_bias
    shift_a, scale_a, gate_a, shift_m, scale_m, gate_m = [
        piece[None, :] for piece in jnp.split(modul, 6)
    ]
    own_tokens = pick(latents, s, 0)
    far_tokens = swap_on(after(pick(latents, 1 - s, 0), qkv_mine[0]), "shard")
    qkv_pieces = [fetch_rest(mine) for mine in qkv_mine]
    fc1_mine = fetch_start(jnp.concatenate([w_fc1, w_proj], axis=1), far_tokens, qkv_mine[1])
    fc1_pieces = fetch_rest(fc1_mine)
    fc2_mine = fetch_start(w_fc2, fc1_mine)
    fc2_beside = swap_on(fc2_mine, "x")
    fc2_across = swap_on(fc2_mine, "core")
    far_cotangent = swap_on(after(pick(cotangent, 1 - s, 0), fc2_mine), "shard")

    full_qkv = [whole_weight(qkv_half(w_qkv, half), qkv_pieces[half]) for half in range(2)]
    tokens = jnp.concatenate([own_tokens, far_tokens], axis=0).astype(jnp.float32)
    norm_a, inv_a = layer_stats(tokens)
    normed = (norm_a * (1.0 + scale_a) + shift_a).astype(jnp.bfloat16)

    def project(half):
        product = jnp.dot(normed, full_qkv[half], preferred_element_type=jnp.float32)
        return (product + qkv_half(qkv_bias, half)).astype(jnp.bfloat16)

    qkv = [project(0), project(1)]
    first = attend(qkv[0], None)
    qkv[1], fc1_mine, first = lax.optimization_barrier((qkv[1], fc1_mine, first))
    attended, log_second = attend(qkv[1], first[0])
    log_total = [first[1], log_second]
    attended, fc2_mine = lax.optimization_barrier((attended, fc2_mine))
    full_proj = whole_weight(w_proj, [p[:, w_fc1.shape[1]:] for p in fc1_pieces])
    full_fc1 = whole_weight(w_fc1, fc1_pieces)
    branch_a = jnp.dot(attended, full_proj, preferred_element_type=jnp.float32) + proj_bias
    resid = tokens + gate_a * branch_a
    norm_m, inv_m = layer_stats(resid)
    mixed = (norm_m * (1.0 + scale_m) + shift_m).astype(jnp.bfloat16)
    pre = jnp.dot(mixed, full_fc1, preferred_element_type=jnp.float32) + fc1_bias
    activated, gelu_back = jax.vjp(partial(jax.nn.gelu, approximate=True), pre)
    hidden = activated.astype(jnp.bfloat16)
    hidden, fc2_beside, fc2_across = lax.optimization_barrier((hidden, fc2_beside, fc2_across))
    fc2_pieces = (fc2_mine, fc2_beside, fc2_across, swap_on(fc2_beside, "core"))
    full_fc2 = whole_weight(w_fc2, fc2_pieces)
    branch_m = jnp.dot(hidden, full_fc2, preferred_element_type=jnp.float32) + fc2_bias
    branch_m, far_cotangent = lax.optimization_barrier((branch_m, far_cotangent))
    cotangents = jnp.concatenate([pick(cotangent, s, 0), far_cotangent], axis=0)
    out = ((resid + gate_m * branch_m) * live).astype(jnp.bfloat16)
    out, hidden = lax.optimization_barrier((out, hidden))
    out_other = swap_on(out[block:], "shard")

    d_out = cotangents.astype(jnp.float32) * live
    d_gate_m = jnp.sum(d_out * branch_m, axis=0)
    d_branch_m = (gate_m * d_out).astype(jnp.bfloat16)
    sum_fc2 = weight_terms(hidden, d_branch_m)
    bias_fc2 = jnp.sum(d_branch_m, axis=0, dtype=jnp.float32)
    d_branch_m = after(d_branch_m, sum_fc2)
    d_pre = gelu_back(contract_last(d_branch_m, full_fc2))[0].astype(jnp.bfloat16)
    keep_fc2, send_fc2 = split_on(over_core(sum_fc2), "shard", 0)
    d_pre, keep_fc2, send_fc2, out_other = lax.optimization_barrier(
        (d_pre, keep_fc2, send_fc2, out_other)
    )
    came_fc2 = swap_on(send_fc2, "shard")
    sum_fc1 = split_terms(mixed, d_pre, width)
    bias_fc1 = jnp.sum(d_pre, axis=0, dtype=jnp.float32)
    d_pre, sum_fc1 = lax.optimization_barrier((d_pre, sum_fc1))
    d_mixed = contract_last(d_pre, full_fc1)
    keep_fc1, send_fc1 = split_on(join_core(sum_fc1), "x", 1)
    d_mixed, keep_fc1, send_fc1 = lax.optimization_barrier((d_mixed, keep_fc1, send_fc1))
    came_fc1 = swap_on(send_fc1, "x")
    d_shift_m = jnp.sum(d_mixed, axis=0)
    d_scale_m = jnp.sum(d_mixed * norm_m, axis=0)
    d_resid = d_out + layer_back(norm_m, inv_m, d_mixed * (1.0 + scale_m))
    d_gate_a = jnp.sum(d_resid * branch_a, axis=0)
    d_branch_a = (gate_a * d_resid).astype(jnp.bfloat16)
    sum_proj = split_terms(attended, d_branch_a, width)
    bias_proj = jnp.sum(d_branch_a, axis=0, dtype=jnp.float32)
    d_attended = contract_last(d_branch_a, full_proj).astype(jnp.bfloat16)
    sum_proj = join_core(sum_proj)
    sum_fc2 = add_low(keep_fc2, came_fc2)
    d_attended, sum_fc2, sum_proj = lax.optimization_barrier((d_attended, sum_fc2, sum_proj))
    d_first = attend_back(qkv[0], attended, d_attended, log_total[0], 0)
    sum_fc1 = add_low(keep_fc1, came_fc1)
    sum_fc2 = over_x(sum_fc2)
    d_attended, sum_fc1, d_first = lax.optimization_barrier((d_attended, sum_fc1, d_first))
    levels = list(range(z_levels()))
    low, high = levels[: len(levels) // 2], levels[len(levels) // 2 :]

    def down(terms, which):
        for level in which:
            terms = z_down(terms, level)
        return terms

    def up(piece, which):
        for level in reversed(which):
            piece = z_up(piece, level)
        return piece

    sum_half = split_terms(normed, d_first, d_first.shape[1])
    d_attended, sum_half, sum_fc2 = lax.optimization_barrier((d_attended, sum_half, sum_fc2))
    d_second = attend_back(qkv[1], attended, d_attended, log_total[1], 1)
    sum_early = jnp.concatenate([sum_proj, join_core(sum_half)], axis=-1)
    sum_fc1 = over_shard(sum_fc1)
    sum_fc2 = down(sum_fc2, low)
    d_second, sum_early, sum_fc2, sum_fc1 = lax.optimization_barrier(
        (d_second, sum_early, sum_fc2, sum_fc1)
    )
    sum_half = split_terms(normed, d_second, d_second.shape[1])
    bias_qv = [jnp.sum(d, axis=0, dtype=jnp.float32) for d in (d_first, d_second)]
    half_width = width // 2
    bias_qv = jnp.concatenate(
        [b[t * half_width : (t + 1) * half_width] for t in (0, 2) for b in bias_qv]
    )
    sum_fc2 = down(sum_fc2, high)
    sum_fc1 = down(sum_fc1, low)
    d_second, sum_half, sum_fc2, sum_fc1 = lax.optimization_barrier(
        (d_second, sum_half, sum_fc2, sum_fc1)
    )
    d_normed = contract_last(d_first, full_qkv[0]) + contract_last(d_second, full_qkv[1])
    keep_late, send_late = split_on(join_core(sum_half), "shard", 0)
    d_normed, keep_late, send_late = lax.optimization_barrier((d_normed, keep_late, send_late))
    came_late = swap_on(send_late, "shard")
    sum_early = over_x(over_shard(sum_early))
    sum_fc2 = up(sum_fc2, high)
    sum_fc1 = down(sum_fc1, high)
    d_shift_a = jnp.sum(d_normed, axis=0)
    d_scale_a = jnp.sum(d_normed * norm_a, axis=0)
    d_modul = jnp.concatenate(
        [d_shift_a, d_scale_a, d_gate_a, d_shift_m, d_scale_m, d_gate_m]
    ).astype(jnp.bfloat16)
    sum_late = add_low(keep_late, came_late)
    output = in_order(out[:block], out_other, "shard")
    d_modul, d_normed, sum_late, sum_early, sum_fc2, sum_fc1 = lax.optimization_barrier(
        (d_modul, d_normed, sum_late, sum_early, sum_fc2, sum_fc1)
    )
    row = jnp.concatenate([d_modul, pick(cond_act, s, 0)])
    terms = [t.reshape(2, -1) for t in (bias_qv, bias_proj, bias_fc1, bias_fc2)]
    terms = jnp.concatenate(terms, axis=1)
    sent = jnp.concatenate([row, pick(terms, 1 - s, 0).astype(jnp.bfloat16)])
    came = swap_on(sent, "shard")
    length = row.shape[0]
    table = in_order(row, came[:length], "shard")
    d_modul_pair = table[:, : d_modul.shape[0]]
    total = pick(terms, s, 0) + came[length:].astype(jnp.float32)

    def grow(table, total, swap):
        both = swap(jnp.concatenate([table.reshape(-1), total.astype(jnp.bfloat16)]))
        size = table.size
        return (
            both[:, :size].reshape(-1, length),
            jnp.sum(both[:, size:].astype(jnp.float32), axis=0),
        )

    sum_late = over_x(sum_late)
    sum_early = down(sum_early, low)
    sum_fc1 = up(sum_fc1, high)
    sum_fc2 = up(sum_fc2, low)
    sum_late, sum_early, sum_fc1, sum_fc2, table, total, d_normed = lax.optimization_barrier(
        (sum_late, sum_early, sum_fc1, sum_fc2, table, total, d_normed)
    )
    pair_fc2 = up_x(sum_fc2)
    sum_late = down(sum_late, low)
    sum_early = down(sum_early, high)
    sum_fc1 = up(sum_fc1, low)
    grad_tokens = d_resid + layer_back(norm_a, inv_a, d_normed * (1.0 + scale_a))
    table, total = grow(table, total, lambda v: in_order(v, swap_on(v, "core"), "core"))
    sum_late, sum_early, sum_fc1, table, total, grad_tokens = lax.optimization_barrier(
        (sum_late, sum_early, sum_fc1, table, total, grad_tokens)
    )
    sum_late = down(sum_late, high)
    sum_early = up(sum_early, high)
    far_grad = swap_on(grad_tokens[block:].astype(jnp.bfloat16), "shard")
    pair_fc1 = up_x(sum_fc1)
    table, total = grow(table, total, lambda v: in_order(v, swap_on(v, "x"), "x"))
    sum_late, sum_early, table, total = lax.optimization_barrier(
        (sum_late, sum_early, table, total)
    )
    sum_late = up(sum_late, high)
    sum_early = up(sum_early, low)
    grad_fc2 = up_core(pair_fc2).astype(jnp.float32)
    for level in low:
        table, total = grow(table, total, lambda v: z_order(v, level))
    sum_late, sum_early, far_grad, table, total, grad_fc2 = lax.optimization_barrier(
        (sum_late, sum_early, far_grad, table, total, grad_fc2)
    )
    sum_late = up(sum_late, low)
    pair_early = up_x(sum_early)
    for level in high:
        table, total = grow(table, total, lambda v: z_order(v, level))
    grad_fc1 = up_core(pair_fc1).astype(jnp.float32)
    sum_late, table, total, grad_fc1 = lax.optimization_barrier(
        (sum_late, table, total, grad_fc1)
    )
    pair_late = up_x(sum_late)
    grad_latents = in_order(grad_tokens[:block], far_grad.astype(jnp.float32), "shard")
    halves = (pair_early[..., width:], pair_late)
    pair_qkv = jnp.concatenate(
        [
            piece[..., t * half_width : (t + 1) * half_width]
            for t in range(3)
            for piece in halves
        ],
        axis=-1,
    )
    grad_proj = up_core(pair_early[..., :width]).astype(jnp.float32)
    grad_qkv = up_core(pair_qkv).astype(jnp.float32)

    d_modul_all, cond_all = table[:, : d_modul.shape[0]], table[:, d_modul.shape[0] :]
    cond_all = lax.dynamic_slice_in_dim(cond_all, s * ada_rows, ada_rows, 1)
    grad_w_ada = lax.dot_general(
        cond_all, d_modul_all, (((0,), (0,)), ((), ())), preferred_element_type=jnp.float32
    )
    ada_length = b_ada.shape[0]
    grad_b_ada = lax.dynamic_slice_in_dim(
        jnp.sum(d_modul_all, axis=0, dtype=jnp.float32), s * ada_length, ada_length, 0
    )
    d_cond = contract_last(d_modul_pair, w_ada)
    d_cond = in_order(d_cond, swap_on(d_cond, "shard"), "shard")
    d_cond_act = jnp.moveaxis(d_cond, 0, 1).reshape(slots, width)
    _, silu_back = jax.vjp(jax.nn.silu, cond_float)
    grad_conditions = silu_back(d_cond_act)[0]
    bias_grads = []
    start = 0
    for bias in biases[1:]:
        size = bias.shape[0]
        bias_grads.append(total[start : start + size])
        start += size
    return (
        output,
        grad_latents,
        grad_conditions,
        grad_w_ada,
        grad_b_ada,
        grad_qkv,
        bias_grads[0],
        grad_proj,
        bias_grads[1],
        grad_fc1,
        bias_grads[2],
        grad_fc2,
        bias_grads[3],
    )


def solution(mesh):
    n_z = mesh.shape["replica"] // 4
    if mesh.shape["shard"] == 2 and n_z & (n_z - 1) == 0 and mesh.shape["replica"] % 4 == 0:
        return pair_solution(mesh)
    return wide_solution(mesh)


def pair_solution(mesh):
    names = mesh.axis_names
    n_replica, n_shard = (mesh.shape["replica"], mesh.shape["shard"])
    devices = mesh.devices.transpose(names.index("replica"), names.index("shard"))
    fine = jax.sharding.Mesh(
        devices.reshape(n_replica // 4, 2, 2, n_shard), ("z", "x", "core", "shard")
    )
    return mapped(pair_shards, fine, ("z", "x", "core"))


def wide_solution(mesh):
    names = mesh.axis_names
    n_replica, n_shard = (mesh.shape["replica"], mesh.shape["shard"])
    devices = mesh.devices.transpose(names.index("replica"), names.index("shard"))
    fine = jax.sharding.Mesh(
        devices.reshape(n_replica // 2, 2, n_shard), ("chip", "core", "shard")
    )
    return mapped(shards, fine, ("chip", "core"))


def mapped(body, fine, replica):
    tokens, weight, vector = (P(replica, "shard", None), P("shard", None), P("shard"))
    return jax.shard_map(
        body,
        mesh=fine,
        in_specs=(tokens, P(replica, None), tokens, P(replica)) + (weight, vector) * 5,
        out_specs=(tokens, tokens, P(replica, None)) + (weight, vector) * 5,
        check_vma=False,
    )
```
